512 devices in a mesh: tile: 32 (over z, y_lo, core), frame: 16 (over x, y_hi).
Axes of the slice: x: 4, y: 8 (y_hi: 4, y_lo: 2; y = y_hi * 2 + y_lo), z: 8, core: 2. Of those that a mesh axis runs over, the one named last changes fastest.
Arguments:
- estimate: float32 [512, 4096], P('tile'), may hold values from -6 to 6
- frames: float32 [16, 256, 2048], P('frame', 'tile'), may hold values from -4 to 4
- shifts: int32 [16, 2], P('frame'), may hold values from -5 to 5, as said below
- blur: float32 [7], replicated, may hold values from 0.2 to 1
Outputs:
- result: float32 [512, 4096], P('tile')
The draws below stay inside these ranges and needn't reach their ends.
Inputs may be any that keep to these rules, and one draw needn't show every extreme that they name: `shifts`: some frame has a row shift of 5 and some frame a column shift of -5.
All inputs are finite; a program needn't handle non-finite values.
Results may differ from the reference program's by a relative error of at most 0.0003.
Values sent between devices are 32-bit elements; how exact they have to be, the bound alone decides.
A program may use at most 128 MiB of HBM per device.

```python
import jax
import jax.numpy as jnp
from jax import lax

W = 4096
FACTOR = 2
RADIUS = 3
SHIFT = 5
WINDOW = 2
ITERS = 2
MARGIN = 8
H = 512
FRAMES = 16


def draw_shifts(key, part):
    values = jax.random.randint(jax.random.fold_in(key, 11), (FRAMES, 2), -SHIFT, SHIFT + 1)
    spots = jax.random.randint(jax.random.fold_in(key, 12), (2,), 0, FRAMES)
    values = values.at[spots[0], 0].set(SHIFT)
    values = values.at[spots[1], 1].set(-SHIFT)
    return values.astype(jnp.int32)


def expand_blocks(field, low_rows, low_cols):
    wider = jnp.repeat(jnp.repeat(field, 4, axis=-2), 16, axis=-1)
    return wider[..., :low_rows, :low_cols]


def draw_frames(key, part):
    low_rows = H // FACTOR
    low_cols = W // FACTOR
    grid_rows = (low_rows + 3) // 4
    grid_cols = (low_cols + 15) // 16
    region = jax.random.randint(jax.random.fold_in(key, 21), (grid_rows, grid_cols), 0, 3)
    magnitude = jax.random.uniform(jax.random.fold_in(key, 22), (FRAMES, grid_rows, grid_cols), jnp.float32, 2.0, 3.5)
    jitter = jnp.clip(0.25 * jax.random.normal(jax.random.fold_in(key, 23), (FRAMES, low_rows, low_cols), jnp.float32), -0.5, 0.5)
    polarity = jnp.where(region == 1, 1.0, -1.0).astype(jnp.float32)
    offset = jnp.where(region == 0, 0.0, polarity * magnitude).astype(jnp.float32)
    values = expand_blocks(offset, low_rows, low_cols) + jitter
    return values.astype(jnp.float32)


def levels(rng, dims, split, low, top_value):
    def one(dim, parts):
        heights = jax.random.uniform(jax.random.fold_in(jax.random.fold_in(rng, 6), dim), (parts,), jnp.float32, low / len(split), top_value / len(split))
        return jnp.repeat(jnp.exp(heights), dims[dim] // parts).reshape((-1,) + (1,) * (len(dims) - dim - 1))

    level = one(*split[0])
    for cut in split[1:]:
        level = level * one(*cut)
    return level


def bell_draw(key, shape, scale, most, split=(), kind=jnp.bfloat16):
    factor_of = levels(key, shape, split, -0.22, 0.18) if split else 1.0
    entries = jax.random.normal(key, shape, jnp.float32) * scale * factor_of
    return jnp.minimum(jnp.maximum(entries, -most), most).astype(kind)


def setup_inputs(seed: int = 0) -> dict:
    key_list = jax.random.split(jax.random.key(seed), 5)
    return {
        "estimate": bell_draw(key_list[0], (H, W), 1.0, 6.0, ((0, 32),), jnp.float32),
        "frames": draw_frames(jax.random.fold_in(key_list[4], 71), 0),
        "shifts": draw_shifts(jax.random.fold_in(key_list[4], 71), 0),
        "blur": jnp.clip(jax.random.uniform(key_list[3], (2 * RADIUS + 1,), jnp.float32, 0.2, 1.0), 0.2, 1.0),
    }


def blur_rows(field, taps, offset):
    count = field.shape[0] - 2 * MARGIN
    total = jnp.zeros((count // FACTOR, field.shape[1]), jnp.float32)
    for tap in range(2 * RADIUS + 1):
        start = (MARGIN + offset + tap - RADIUS).astype(jnp.int32)
        piece = lax.dynamic_slice_in_dim(field, start, count, 0)
        total = total + taps[tap] * piece.reshape(count // FACTOR, FACTOR, field.shape[1])[:, 0]
    return total

def forward(image, taps, down_shift, side_shift):
    padded = jnp.pad(image, MARGIN)
    rows_done = blur_rows(padded, taps, down_shift)
    return blur_rows(rows_done.T, taps, side_shift).T

def prior_term(image):
    height, width = image.shape
    padded = jnp.pad(image, WINDOW)
    total = jnp.zeros_like(image)
    for down_off in range(-WINDOW, WINDOW + 1):
        for side_off in range(-WINDOW, WINDOW + 1):
            if down_off == 0 and side_off == 0:
                continue
            near = padded[WINDOW + down_off:WINDOW + down_off + height, WINDOW + side_off:WINDOW + side_off + width]
            slope = jnp.tanh((image - near) / 0.5)
            spread = jnp.pad(slope, WINDOW)
            behind = spread[WINDOW - down_off:WINDOW - down_off + height, WINDOW - side_off:WINDOW - side_off + width]
            total = total + 0.7 ** (abs(down_off) + abs(side_off)) * (slope - behind)
    return total

def reference(estimate, frames, shifts, blur):
    taps = blur / jnp.sum(blur)
    image = estimate
    for step in range(ITERS):

        def add_frame(total, item):
            frame, shift = item
            pred, pullback = jax.vjp(lambda field: forward(field, taps, shift[0], shift[1]), image)
            return (total + pullback(jnp.tanh(pred - frame))[0], None)
        data, unused = lax.scan(add_frame, jnp.zeros_like(image), (frames, shifts))
        image = image - 0.1 * (data + 0.05 * prior_term(image))
    return image
```

```python
import functools

import jax
import jax.numpy as jnp
from jax import lax
from jax.experimental import pallas as pl
from jax.experimental.pallas import tpu as pltpu
from jax.sharding import PartitionSpec as P

RADIUS = 3
TAPS = 2 * RADIUS + 1
WINDOW = 2
REACH = 8
OFFS = 2 * REACH + 1
SIDE = 4
CHUNK = 256
LOW = CHUNK // 2
EDGE = 12
ROWS = 16
BAND = 2 * ROWS
SPAN = 640
KDIM = 640
MESH = pl.DeviceIdType.MESH
F32 = jnp.float32
BF16 = jnp.bfloat16


def iota(shape, axis):
    return lax.broadcasted_iota(jnp.int32, shape, axis)


def three(value):
    high = value.astype(BF16)
    rest = value - high.astype(F32)
    middle = rest.astype(BF16)
    low = (rest - middle.astype(F32)).astype(BF16)
    return jnp.concatenate([high, middle, low], axis=0)


def pick(value, table):
    rows = value.shape[0]
    out = jnp.dot(three(value), table, preferred_element_type=F32)
    return out[:rows] + out[rows : 2 * rows] + out[2 * rows :]


def left(value, amount):
    width = value.shape[1]
    return value if amount % width == 0 else pltpu.roll(value, (-amount) % width, 1)


def kernel(
    tiles, est, frames, shifts, blur, out,
    xw, fr, ys, yb, fb, sb, xs, px, pg, xb, aa, af, hh, d1, r1, d2, r2, pr,
    load_sem, ysend, yrecv, hsend, hrecv, fsend, frecv, ssend, srecv,
    e1send, e1recv, e2send, e2recv, gsend, grecv,
):
    t = lax.axis_index("tile")
    f = lax.axis_index("frame")
    x = f // SIDE
    y = f % SIDE
    c = SIDE * y + x
    last = SIDE * SIDE - 1
    at_low = (last - c) // last
    at_high = c // last
    start = pl.multiple_of(128 * (2 * c - 1 + at_low - at_high), 128)
    lane0 = pl.multiple_of(128 * (1 + at_low - at_high), 128)
    up = lax.rem(t + tiles - 1, tiles)
    down = lax.rem(t + 1, tiles)

    def ypeer(e):
        return {"frame": SIDE * x + lax.rem(y + e, SIDE)}

    def xpeer(e):
        return {"frame": SIDE * lax.rem(x + e, SIDE) + y}

    def remote(src, dst, send, recv, device):
        return pltpu.make_async_remote_copy(
            src_ref=src, dst_ref=dst, send_sem=send, recv_sem=recv, device_id=device, device_id_type=MESH
        )

    window = est.at[:, pl.ds(start, 512)]
    load_f = pltpu.make_async_copy(frames.at[0], fr, load_sem.at[0])
    load_x = pltpu.make_async_copy(window, xw.at[pl.ds(ROWS, ROWS), pl.ds(lane0, 512)], load_sem.at[1])
    load_f.start()
    load_x.start()

    barrier = pltpu.get_barrier_semaphore()
    for e in range(1, SIDE):
        pl.semaphore_signal(barrier, inc=1, device_id=ypeer(e), device_id_type=MESH)
        pl.semaphore_signal(barrier, inc=1, device_id=xpeer(e), device_id_type=MESH)
    pl.semaphore_signal(barrier, inc=1, device_id={"tile": up}, device_id_type=MESH)
    pl.semaphore_signal(barrier, inc=1, device_id={"tile": down}, device_id_type=MESH)

    load_f.wait()
    lane = iota((8, 128), 1)
    sub = iota((8, 128), 0)
    shift_tile = jnp.where(
        sub < 4, jnp.full((8, 128), shifts[0, 0].astype(F32)), jnp.full((8, 128), shifts[0, 1].astype(F32))
    )
    before = jnp.zeros((8, 128), F32)
    per_span = SIDE * LOW // 128
    for tile in range(SIDE * per_span + 1):
        if tile < SIDE * per_span:
            rolled = pltpu.roll(fr[:, 128 * tile : 128 * tile + 128], EDGE, 1)
        else:
            rolled = jnp.zeros((8, 128), F32)
        moved = jnp.where(lane < EDGE, before, rolled)
        before = rolled
        if tile < SIDE * per_span:
            at = 128 * (tile % per_span)
            ys[tile // per_span, :, at : at + 128] = moved
        if tile and tile % per_span == 0:
            ys[tile // per_span - 1, :, SPAN - 128 : SPAN] = jnp.where(lane < 2 * EDGE, moved, shift_tile)
    yb[0] = ys[y]

    pl.semaphore_wait(barrier, 2 * SIDE)

    started = []

    def go(copy):
        copy.start()
        started.append(copy)
        return copy

    ycopies = {}
    for e in (2, 1, 3):
        target = lax.rem(y + e, SIDE)
        ycopies[e] = go(remote(ys.at[target], yb.at[e], ysend.at[e], yrecv.at[e], ypeer(e)))
    halo_down = go(
        remote(window, xw.at[pl.ds(0, ROWS), pl.ds(lane0, 512)], hsend.at[0], hrecv.at[0], {"tile": down})
    )
    halo_up = go(
        remote(window, xw.at[pl.ds(2 * ROWS, ROWS), pl.ds(lane0, 512)], hsend.at[1], hrecv.at[1], {"tile": up})
    )
    fcopies = {}
    scopies = {}

    def forward(ey):
        for ex in (2, 1, 3):
            target = pl.multiple_of(LOW * lax.rem(x + ex, SIDE), LOW)
            slot = SIDE * ex + ey
            scopies[slot] = go(
                remote(yb.at[ey, :, pl.ds(SPAN - 128, 128)], sb.at[ex, ey], ssend.at[slot], srecv.at[slot], xpeer(ex))
            )
            fcopies[slot] = go(
                remote(yb.at[ey, :, pl.ds(target, 256)], fb.at[ex, ey], fsend.at[slot], frecv.at[slot], xpeer(ex))
            )
        fb[0, ey] = yb[ey, :, pl.ds(pl.multiple_of(LOW * x, LOW), 256)]
        sb[0, ey] = yb[ey, :, pl.ds(SPAN - 128, 128)]

    forward(0)

    high_cols = CHUNK * SIDE * SIDE
    load_x.wait()
    halo_down.wait_recv()
    halo_up.wait_recv()
    row = ROWS * t - ROWS + iota((3 * ROWS, 512), 0)
    col = CHUNK * c - 128 + iota((3 * ROWS, 512), 1)
    inside = (row >= 0) & (row < ROWS * tiles) & (col >= 0) & (col < high_cols)
    raw = jnp.where(inside, xw[:, 128:640], 0.0)
    lane_in = iota((512, 256), 0)
    lane_out = iota((512, 256), 1)
    for phase in range(2):
        table = jnp.where(lane_in == 96 + phase + 2 * lane_out, 1.0, 0.0).astype(BF16)
        xs[phase] = pick(raw, table)

    row = ROWS * t - ROWS + iota((3 * ROWS, 256), 0)
    col = CHUNK * c - 32 + 2 * iota((3 * ROWS, 256), 1)
    inside = (row >= 0) & (row < ROWS * tiles) & (col >= 0) & (col < high_cols)
    gain = jnp.where(inside, 2.0, 1.0)
    pg[0] = left(gain, -1)
    pg[1] = gain
    pg[2] = left(gain, 1)

    def stage_model(lo):
        for off in range(OFFS):
            xb[BAND * off : BAND * off + BAND] = left(xs[off % 2, lo : lo + BAND], off // 2)

    def stage_prior(lo, count):
        for phase in range(2):
            double = 2.0 * xs[phase, lo : lo + count]
            px[3 * phase, lo : lo + count] = left(double, -1)
            px[3 * phase + 1, lo : lo + count] = double
            px[3 * phase + 2, lo : lo + count] = left(double, 1)

    def prior(phase, lo, count):
        centre = px[3 * phase + 1, lo : lo + count]
        total = jnp.zeros((count, 256), F32)
        for side in range(-WINDOW, WINDOW + 1):
            other = (phase + side) % 2
            lanes = (phase + side - other) // 2 + 1
            for down_off in range(-WINDOW, WINDOW + 1):
                if down_off == 0 and side == 0:
                    continue
                rows = slice(lo + down_off, lo + down_off + count)
                weight = 0.7 ** (abs(down_off) + abs(side))
                slope = jnp.tanh(centre - px[3 * other + lanes, rows])
                total = total + (weight * slope) * pg[lanes, rows]
        return total

    xb[OFFS * BAND : KDIM] = jnp.zeros((KDIM - OFFS * BAND, 256), F32)
    aa[OFFS * BAND : KDIM] = jnp.zeros((KDIM - OFFS * BAND, 128), F32)
    stage_model(REACH)
    stage_prior(0, 3 * ROWS)

    for ey in (1, 3, 2):
        ycopies[ey].wait_recv()
        forward(ey)

    for phase in range(2):
        pr[phase] = xs[phase, REACH : REACH + BAND] - 0.005 * prior(phase, REACH, BAND)

    for copy in scopies.values():
        copy.wait_recv()
    tile = jnp.zeros((8, 128), F32)
    for slot in range(SIDE * SIDE):
        piece = sb[slot // SIDE, slot % SIDE]
        if slot < 3:
            piece = pltpu.roll(piece, 64, 1)
        tile = jnp.where(lane // 8 == slot, piece, tile)
    blur_sum = blur[0]
    for tap in range(1, TAPS):
        blur_sum = blur_sum + blur[tap]
    scale = jnp.full((1, 128), blur_sum)
    taps = [jnp.full((1, 128), blur[tap]) / scale for tap in range(TAPS)]

    def tap_at(distance):
        total = jnp.zeros(distance.shape, F32)
        for tap in range(TAPS):
            total = jnp.where(distance == float(tap - RADIUS), jnp.broadcast_to(taps[tap], distance.shape), total)
        return total

    place = (iota((BAND, 128), 0) - REACH - 2 * (iota((BAND, 128), 1) % 8)).astype(F32)
    by_row = tap_at(place - tile[0:1])
    by_col = tap_at((iota((24, 128), 0) - REACH).astype(F32) - tile[4:5])
    for off in range(OFFS):
        aa[BAND * off : BAND * off + BAND] = by_row * by_col[off : off + 1]
    for block in range(KDIM // 128):
        af[:, 128 * block : 128 * block + 128] = aa[128 * block : 128 * block + 128].T

    low = LOW * c - EDGE + iota((128, 256), 1)
    live = (low >= 0) & (low < LOW * SIDE * SIDE)

    def misfits():
        pred = jnp.dot(af[...], xb[...], precision=lax.Precision.HIGH, preferred_element_type=F32)
        return pred

    def adjoint(pred):
        gap = jnp.where(live, jnp.tanh(pred - fb[...].reshape(128, 256)), 0.0)
        hh[...] = jnp.dot(
            aa[: OFFS * BAND], gap, precision=lax.Precision.HIGH, preferred_element_type=F32
        )

    pred = misfits()
    for copy in fcopies.values():
        copy.wait_recv()
    adjoint(pred)
    for phase in range(2):
        total = jnp.zeros((BAND, 256), F32)
        for off in range(phase, OFFS, 2):
            total = total + left(hh[BAND * off : BAND * off + BAND], -(off // 2))
        d1[phase] = total
    to_up = go(remote(d1.at[:, pl.ds(0, ROWS)], r1.at[:, pl.ds(ROWS, ROWS)], e1send.at[0], e1recv.at[0], {"tile": up}))
    to_down = go(
        remote(d1.at[:, pl.ds(ROWS, ROWS)], r1.at[:, pl.ds(0, ROWS)], e1send.at[1], e1recv.at[1], {"tile": down})
    )
    reach_row = ROWS * t - REACH + iota((BAND, 256), 0)
    edge_row = (reach_row < REACH) | (reach_row >= ROWS * tiles - REACH)
    within = pg[1, REACH : REACH + BAND] > 1.5
    to_up.wait_recv()
    to_down.wait_recv()
    for phase in range(2):
        theirs = jnp.where(edge_row, 0.0, r1[phase])
        xs[phase, REACH : REACH + BAND] = jnp.where(within, pr[phase] - 0.1 * (d1[phase] + theirs), 0.0)

    stage_model(REACH)
    adjoint(misfits())
    both = []
    for phase in range(2):
        total = jnp.zeros((BAND, 128), F32)
        for off in range(phase, OFFS, 2):
            total = total + left(hh[BAND * off : BAND * off + BAND], ROWS - off // 2)[:, :128]
        d2[0, phase] = total[:REACH]
        d2[1, phase] = total[3 * REACH :]
        both.append(total[REACH : 3 * REACH])
    to_up2 = go(remote(d2.at[0], r2.at[1], e2send.at[0], e2recv.at[0], {"tile": up}))
    to_down2 = go(remote(d2.at[1], r2.at[0], e2send.at[1], e2recv.at[1], {"tile": down}))

    stage_prior(REACH, BAND)
    for phase in range(2):
        mine = xs[phase, ROWS : 2 * ROWS] - 0.005 * prior(phase, ROWS, ROWS)
        both[phase] = left(mine, ROWS)[:, :128] - 0.1 * both[phase]
    lane_in = iota((CHUNK, CHUNK), 0)
    lane_out = iota((CHUNK, CHUNK), 1)
    table = jnp.where(lane_out == jnp.where(lane_in < LOW, 2 * lane_in, 2 * lane_in - CHUNK + 1), 1.0, 0.0).astype(BF16)
    own_row = ROWS * t + iota((ROWS, LOW), 0)
    edge_row = (own_row < REACH) | (own_row >= ROWS * tiles - REACH)
    to_up2.wait_recv()
    to_down2.wait_recv()
    halves = []
    for phase in range(2):
        theirs = jnp.concatenate([r2[0, phase], r2[1, phase]], axis=0)
        halves.append(both[phase] - 0.1 * jnp.where(edge_row, 0.0, theirs))
    result = pick(jnp.concatenate(halves, axis=1), table)

    def chunk_of(ey):
        source = SIDE * lax.rem(y + SIDE - ey, SIDE) + x
        return out.at[:, pl.ds(pl.multiple_of(CHUNK * source, CHUNK), CHUNK)]

    out[:, pl.ds(pl.multiple_of(CHUNK * c, CHUNK), CHUNK)] = result
    gathers = {}
    for e in (2, 1, 3):
        gathers[e] = go(remote(chunk_of(0), chunk_of(0), gsend.at[e], grecv.at[e], ypeer(e)))

    def spread(ey):
        for ex in (2, 1, 3):
            slot = SIDE * ex + ey
            gathers[slot] = go(remote(chunk_of(ey), chunk_of(ey), gsend.at[slot], grecv.at[slot], xpeer(ex)))

    spread(0)
    for ey in (1, 3, 2):
        gathers[ey].wait_recv()
        spread(ey)
    for slot, copy in gathers.items():
        if slot >= SIDE:
            copy.wait_recv()
    for copy in started:
        copy.wait_send()


def local(tiles, estimate, frames, shifts, blur):
    vmem = lambda *shape: pltpu.VMEM(shape, F32)
    dma = lambda n: pltpu.SemaphoreType.DMA((n,))
    both = SIDE * SIDE
    return pl.pallas_call(
        functools.partial(kernel, tiles),
        out_shape=jax.ShapeDtypeStruct(estimate.shape, F32),
        in_specs=[
            pl.BlockSpec(memory_space=pl.ANY),
            pl.BlockSpec(memory_space=pl.ANY),
            pl.BlockSpec(memory_space=pltpu.SMEM),
            pl.BlockSpec(memory_space=pltpu.SMEM),
        ],
        out_specs=pl.BlockSpec(memory_space=pltpu.VMEM),
        scratch_shapes=[
            vmem(3 * ROWS, 768),
            vmem(8, SIDE * SIDE * LOW),
            vmem(SIDE, 8, SPAN),
            vmem(SIDE, 8, SPAN),
            vmem(SIDE, SIDE, 8, 256),
            vmem(SIDE, SIDE, 8, 128),
            vmem(2, 3 * ROWS, 256),
            vmem(6, 3 * ROWS, 256),
            vmem(3, 3 * ROWS, 256),
            vmem(KDIM, 256),
            vmem(KDIM, 128),
            vmem(128, KDIM),
            vmem(OFFS * BAND, 256),
            vmem(2, BAND, 256),
            vmem(2, BAND, 256),
            vmem(2, 2, REACH, 128),
            vmem(2, 2, REACH, 128),
            vmem(2, BAND, 256),
            dma(2), dma(SIDE), dma(SIDE), dma(2), dma(2), dma(both), dma(both), dma(both), dma(both),
            dma(2), dma(2), dma(2), dma(2), dma(both), dma(both),
        ],
        compiler_params=pltpu.CompilerParams(collective_id=0, has_side_effects=True),
    )(estimate, frames, shifts, blur)


def solution(mesh):
    placed = (P("tile", None), P("frame", "tile", None), P("frame", None), P())
    return jax.shard_map(
        functools.partial(local, mesh.shape["tile"]),
        mesh=mesh, in_specs=placed, out_specs=P("tile", None), check_vma=False,
    )
```

```python
import functools

import jax
import jax.numpy as jnp
from jax import lax
from jax.experimental import pallas as pl
from jax.experimental.pallas import tpu as pltpu
from jax.sharding import PartitionSpec as P

RADIUS = 3
TAPS = 2 * RADIUS + 1
WINDOW = 2
REACH = 8
OFFS = 2 * REACH + 1
SIDE = 4
CHUNK = 256
LOW = CHUNK // 2
EDGE = 12
ROWS = 16
BAND = 2 * ROWS
SPAN = 768
PIECE = 384
KDIM = 640
MESH = pl.DeviceIdType.MESH
F32 = jnp.float32
BF16 = jnp.bfloat16


def iota(shape, axis):
    return lax.broadcasted_iota(jnp.int32, shape, axis)


def three(value):
    high = value.astype(BF16)
    rest = value - high.astype(F32)
    middle = rest.astype(BF16)
    low = (rest - middle.astype(F32)).astype(BF16)
    return jnp.concatenate([high, middle, low], axis=0)


def pick(value, table):
    rows = value.shape[0]
    out = jnp.dot(three(value), table, preferred_element_type=F32)
    return out[:rows] + out[rows : 2 * rows] + out[2 * rows :]


def left(value, amount):
    width = value.shape[1]
    return value if amount % width == 0 else pltpu.roll(value, (-amount) % width, 1)


def kernel(
    tiles, est, frames, shifts, blur, out,
    taps_in, xw, yb, fb, fs, sy, sx, xs, px, pg, xb, aa, af, hh, d1, r1, d2, r2, pr,
    load_sem, ysend, yrecv, hsend, hrecv, fsend, frecv, usend, urecv, ssend, srecv,
    e1send, e1recv, e2send, e2recv, gsend, grecv,
):
    t = lax.axis_index("tile")
    f = lax.axis_index("frame")
    x = f // SIDE
    y = f % SIDE
    c = SIDE * y + x
    last = SIDE * SIDE - 1
    at_low = (last - c) // last
    at_high = c // last
    start = pl.multiple_of(128 * (2 * c - 1 + at_low - at_high), 128)
    lane0 = pl.multiple_of(128 * (1 + at_low - at_high), 128)
    up = lax.rem(t + tiles - 1, tiles)
    down = lax.rem(t + 1, tiles)

    def ypeer(e):
        return {"frame": SIDE * x + lax.rem(y + e, SIDE)}

    def xpeer(e):
        return {"frame": SIDE * lax.rem(x + e, SIDE) + y}

    def remote(src, dst, send, recv, device):
        return pltpu.make_async_remote_copy(
            src_ref=src, dst_ref=dst, send_sem=send, recv_sem=recv, device_id=device, device_id_type=MESH
        )

    def across_tiles(above, below):
        has_above, has_below = t > 0, t < tiles - 1

        class Pair:
            def start(self):
                pl.when(has_above)(above.start)
                pl.when(has_below)(below.start)

            def wait_recv(self):
                pl.when(has_above)(below.wait_recv)
                pl.when(has_below)(above.wait_recv)

            def wait_send(self):
                pl.when(has_above)(above.wait_send)
                pl.when(has_below)(below.wait_send)

        return Pair()

    def span(target):
        edge = (SIDE - 1 - target) // (SIDE - 1) - target // (SIDE - 1)
        source = pl.multiple_of(128 * (SIDE * target - 1 + edge), 128)
        return frames.at[0, :, pl.ds(source, SPAN)], pl.ds(pl.multiple_of(128 * (1 + edge), 128), SPAN)

    window = est.at[:, pl.ds(start, 512)]
    own_span, own_lanes = span(y)
    load_f = pltpu.make_async_copy(own_span, yb.at[0, :, own_lanes], load_sem.at[0])
    load_x = pltpu.make_async_copy(window, xw.at[pl.ds(ROWS, ROWS), pl.ds(lane0, 512)], load_sem.at[1])
    load_s = pltpu.make_async_copy(shifts, sy.at[0], load_sem.at[2])
    load_b = pltpu.make_async_copy(blur, taps_in, load_sem.at[3])

    barrier = pltpu.get_barrier_semaphore()

    def greet(device):
        pl.semaphore_signal(barrier, inc=1, device_id=device, device_id_type=MESH)

    for e in (2, 1, 3):
        greet(ypeer(e))
    for e in (2, 1, 3):
        greet(xpeer(e))
    pl.when(t > 0)(lambda: greet({"tile": up}))
    pl.when(t < tiles - 1)(lambda: greet({"tile": down}))
    load_f.start()
    load_x.start()
    load_s.start()
    load_b.start()
    pl.semaphore_wait(barrier, 2 * SIDE - 1 + (t + tiles - 1) // tiles - (t + 1) // tiles)

    started = []

    def go(copy):
        copy.start()
        started.append(copy)
        return copy

    ycopies = {}
    ucopies = {}
    for e in (2, 1, 3):
        source, lanes = span(lax.rem(y + e, SIDE))
        ucopies[e] = go(remote(shifts, sy.at[e], usend.at[e], urecv.at[e], ypeer(e)))
        ycopies[e] = go(remote(source, yb.at[e, :, lanes], ysend.at[e], yrecv.at[e], ypeer(e)))
    halo = go(
        across_tiles(
            remote(window, xw.at[pl.ds(2 * ROWS, ROWS), pl.ds(lane0, 512)], hsend.at[0], hrecv.at[1], {"tile": up}),
            remote(window, xw.at[pl.ds(0, ROWS), pl.ds(lane0, 512)], hsend.at[1], hrecv.at[0], {"tile": down}),
        )
    )
    fcopies = {}
    scopies = {}

    def forward(ey):
        for ex in (2, 1, 3):
            target = pl.multiple_of(LOW * lax.rem(x + ex, SIDE) + 128, 128)
            slot = SIDE * ex + ey
            scopies[slot] = go(remote(sy.at[ey], sx.at[ex, ey], ssend.at[slot], srecv.at[slot], xpeer(ex)))
            fcopies[slot] = go(
                remote(yb.at[ey, :, pl.ds(target, PIECE)], fb.at[ex, ey], fsend.at[slot], frecv.at[slot], xpeer(ex))
            )

    load_f.wait()
    load_s.wait()
    forward(0)

    high_cols = CHUNK * SIDE * SIDE
    load_x.wait()
    halo.wait_recv()
    row = ROWS * t - ROWS + iota((3 * ROWS, 512), 0)
    col = CHUNK * c - 128 + iota((3 * ROWS, 512), 1)
    inside = (row >= 0) & (row < ROWS * tiles) & (col >= 0) & (col < high_cols)
    raw = jnp.where(inside, xw[:, 128:640], 0.0)
    lane_in = iota((512, 256), 0)
    lane_out = iota((512, 256), 1)
    for phase in range(2):
        table = jnp.where(lane_in == 96 + phase + 2 * lane_out, 1.0, 0.0).astype(BF16)
        xs[phase] = pick(raw, table)

    row = ROWS * t - ROWS + iota((3 * ROWS, 256), 0)
    col = CHUNK * c - 32 + 2 * iota((3 * ROWS, 256), 1)
    inside = (row >= 0) & (row < ROWS * tiles) & (col >= 0) & (col < high_cols)
    gain = jnp.where(inside, 2.0, 1.0)
    pg[0] = left(gain, -1)
    pg[1] = gain
    pg[2] = left(gain, 1)

    def stage_model(lo):
        for off in range(OFFS):
            xb[BAND * off : BAND * off + BAND] = left(xs[off % 2, lo : lo + BAND], off // 2)

    def stage_prior(lo, count):
        for phase in range(2):
            double = 2.0 * xs[phase, lo : lo + count]
            px[3 * phase, lo : lo + count] = left(double, -1)
            px[3 * phase + 1, lo : lo + count] = double
            px[3 * phase + 2, lo : lo + count] = left(double, 1)

    def prior(phase, lo, count):
        centre = px[3 * phase + 1, lo : lo + count]
        total = jnp.zeros((count, 256), F32)
        for side in range(-WINDOW, WINDOW + 1):
            other = (phase + side) % 2
            lanes = (phase + side - other) // 2 + 1
            for down_off in range(-WINDOW, WINDOW + 1):
                if down_off == 0 and side == 0:
                    continue
                rows = slice(lo + down_off, lo + down_off + count)
                weight = 0.7 ** (abs(down_off) + abs(side))
                slope = jnp.tanh(centre - px[3 * other + lanes, rows])
                total = total + (weight * slope) * pg[lanes, rows]
        return total

    xb[OFFS * BAND : KDIM] = jnp.zeros((KDIM - OFFS * BAND, 256), F32)
    aa[OFFS * BAND : KDIM] = jnp.zeros((KDIM - OFFS * BAND, 128), F32)
    stage_model(REACH)
    stage_prior(0, 3 * ROWS)

    for ey in (1, 3, 2):
        ucopies[ey].wait_recv()
        ycopies[ey].wait_recv()
        forward(ey)

    for phase in range(2):
        pr[phase] = xs[phase, REACH : REACH + BAND] - 0.005 * prior(phase, REACH, BAND)

    for copy in scopies.values():
        copy.wait_recv()
    frame = iota((1, 128), 1) // 8
    down_shift = jnp.zeros((1, 128), jnp.int32)
    side_shift = jnp.zeros((1, 128), jnp.int32)
    for slot in range(SIDE * SIDE):
        ex, ey = slot // SIDE, slot % SIDE
        pair = sx[ex, ey] if ex else sy[ey]
        down_shift = jnp.where(frame == slot, pair[0:1, 0:1], down_shift)
        side_shift = jnp.where(frame == slot, pair[0:1, 1:2], side_shift)
    load_b.wait()
    blur_sum = taps_in[0]
    for tap in range(1, TAPS):
        blur_sum = blur_sum + taps_in[tap]
    scale = jnp.full((1, 128), blur_sum)
    taps = [jnp.full((1, 128), taps_in[tap]) / scale for tap in range(TAPS)]

    def tap_at(distance):
        total = jnp.zeros(distance.shape, F32)
        for tap in range(TAPS):
            total = jnp.where(distance == tap - RADIUS, jnp.broadcast_to(taps[tap], distance.shape), total)
        return total

    place = iota((BAND, 128), 0) - REACH - 2 * (iota((BAND, 128), 1) % 8)
    by_row = tap_at(place - down_shift)
    by_col = tap_at(iota((24, 128), 0) - REACH - side_shift)
    for off in range(OFFS):
        aa[BAND * off : BAND * off + BAND] = by_row * by_col[off : off + 1]
    for block in range(KDIM // 128):
        af[:, 128 * block : 128 * block + 128] = aa[128 * block : 128 * block + 128].T

    low = LOW * c - EDGE + iota((128, 256), 1)
    live = (low >= 0) & (low < LOW * SIDE * SIDE)

    def misfits():
        pred = jnp.dot(af[...], xb[...], precision=lax.Precision.HIGH, preferred_element_type=F32)
        return pred

    def adjoint(pred):
        gap = jnp.where(live, jnp.tanh(pred - fs[...]), 0.0)
        hh[...] = jnp.dot(
            aa[: OFFS * BAND], gap, precision=lax.Precision.HIGH, preferred_element_type=F32
        )

    pred = misfits()
    for slot in range(SIDE * SIDE):
        ex, ey = slot // SIDE, slot % SIDE
        if ex:
            fcopies[slot].wait_recv()
            piece = fb[ex, ey]
        else:
            piece = yb[ey, :, pl.ds(pl.multiple_of(LOW * x + 128, 128), PIECE)]
        fs[8 * slot : 8 * slot + 8] = left(piece, 128 - EDGE)[:, :256]
    adjoint(pred)
    for phase in range(2):
        total = jnp.zeros((BAND, 256), F32)
        for off in range(phase, OFFS, 2):
            total = total + left(hh[BAND * off : BAND * off + BAND], -(off // 2))
        d1[phase] = total
    first = go(
        across_tiles(
            remote(d1.at[:, pl.ds(0, ROWS)], r1.at[:, pl.ds(ROWS, ROWS)], e1send.at[0], e1recv.at[1], {"tile": up}),
            remote(d1.at[:, pl.ds(ROWS, ROWS)], r1.at[:, pl.ds(0, ROWS)], e1send.at[1], e1recv.at[0], {"tile": down}),
        )
    )
    reach_row = ROWS * t - REACH + iota((BAND, 256), 0)
    edge_row = (reach_row < REACH) | (reach_row >= ROWS * tiles - REACH)
    within = pg[1, REACH : REACH + BAND] > 1.5
    first.wait_recv()
    for phase in range(2):
        theirs = jnp.where(edge_row, 0.0, r1[phase])
        xs[phase, REACH : REACH + BAND] = jnp.where(within, pr[phase] - 0.1 * (d1[phase] + theirs), 0.0)

    stage_model(REACH)
    adjoint(misfits())
    both = []
    for phase in range(2):
        total = jnp.zeros((BAND, 128), F32)
        for off in range(phase, OFFS, 2):
            total = total + left(hh[BAND * off : BAND * off + BAND], ROWS - off // 2)[:, :128]
        d2[0, phase] = total[:REACH]
        d2[1, phase] = total[3 * REACH :]
        both.append(total[REACH : 3 * REACH])
    second = go(
        across_tiles(
            remote(d2.at[0], r2.at[1], e2send.at[0], e2recv.at[1], {"tile": up}),
            remote(d2.at[1], r2.at[0], e2send.at[1], e2recv.at[0], {"tile": down}),
        )
    )

    stage_prior(REACH, BAND)
    for phase in range(2):
        mine = xs[phase, ROWS : 2 * ROWS] - 0.005 * prior(phase, ROWS, ROWS)
        both[phase] = left(mine, ROWS)[:, :128] - 0.1 * both[phase]
    lane_in = iota((CHUNK, CHUNK), 0)
    lane_out = iota((CHUNK, CHUNK), 1)
    table = jnp.where(lane_out == jnp.where(lane_in < LOW, 2 * lane_in, 2 * lane_in - CHUNK + 1), 1.0, 0.0).astype(BF16)
    own_row = ROWS * t + iota((ROWS, LOW), 0)
    edge_row = (own_row < REACH) | (own_row >= ROWS * tiles - REACH)
    second.wait_recv()
    halves = []
    for phase in range(2):
        theirs = jnp.concatenate([r2[0, phase], r2[1, phase]], axis=0)
        halves.append(both[phase] - 0.1 * jnp.where(edge_row, 0.0, theirs))
    result = pick(jnp.concatenate(halves, axis=1), table)

    def chunk_of(ey):
        source = SIDE * lax.rem(y + SIDE - ey, SIDE) + x
        return out.at[:, pl.ds(pl.multiple_of(CHUNK * source, CHUNK), CHUNK)]

    out[:, pl.ds(pl.multiple_of(CHUNK * c, CHUNK), CHUNK)] = result
    gathers = {}
    for e in (2, 1, 3):
        gathers[e] = go(remote(chunk_of(0), chunk_of(0), gsend.at[e], grecv.at[e], ypeer(e)))

    def spread(ey):
        for ex in (2, 1, 3):
            slot = SIDE * ex + ey
            gathers[slot] = go(remote(chunk_of(ey), chunk_of(ey), gsend.at[slot], grecv.at[slot], xpeer(ex)))

    spread(0)
    for ey in (1, 3, 2):
        gathers[ey].wait_recv()
        spread(ey)
    for slot, copy in gathers.items():
        if slot >= SIDE:
            copy.wait_recv()
    for copy in started:
        copy.wait_send()


def local(tiles, estimate, frames, shifts, blur):
    vmem = lambda *shape: pltpu.VMEM(shape, F32)
    dma = lambda n: pltpu.SemaphoreType.DMA((n,))
    both = SIDE * SIDE
    return pl.pallas_call(
        functools.partial(kernel, tiles),
        out_shape=jax.ShapeDtypeStruct(estimate.shape, F32),
        in_specs=[pl.BlockSpec(memory_space=pl.ANY)] * 4,
        out_specs=pl.BlockSpec(memory_space=pltpu.VMEM),
        scratch_shapes=[
            pltpu.SMEM((TAPS,), F32),
            vmem(3 * ROWS, 768),
            vmem(SIDE, 8, SPAN + 256),
            vmem(SIDE, SIDE, 8, PIECE),
            vmem(128, 256),
            pltpu.VMEM((SIDE, 1, 2), jnp.int32),
            pltpu.VMEM((SIDE, SIDE, 1, 2), jnp.int32),
            vmem(2, 3 * ROWS, 256),
            vmem(6, 3 * ROWS, 256),
            vmem(3, 3 * ROWS, 256),
            vmem(KDIM, 256),
            vmem(KDIM, 128),
            vmem(128, KDIM),
            vmem(OFFS * BAND, 256),
            vmem(2, BAND, 256),
            vmem(2, BAND, 256),
            vmem(2, 2, REACH, 128),
            vmem(2, 2, REACH, 128),
            vmem(2, BAND, 256),
            dma(4), dma(SIDE), dma(SIDE), dma(2), dma(2), dma(both), dma(both), dma(SIDE), dma(SIDE), dma(both), dma(both),
            dma(2), dma(2), dma(2), dma(2), dma(both), dma(both),
        ],
        compiler_params=pltpu.CompilerParams(collective_id=0, has_side_effects=True),
    )(estimate, frames, shifts, blur)


def solution(mesh):
    placed = (P("tile", None), P("frame", "tile", None), P("frame", None), P())
    return jax.shard_map(
        functools.partial(local, mesh.shape["tile"]),
        mesh=mesh, in_specs=placed, out_specs=P("tile", None), check_vma=False,
    )
```

```python
import functools

import jax
import jax.numpy as jnp
from jax import lax
from jax.experimental import pallas as pl
from jax.experimental.pallas import tpu as pltpu
from jax.sharding import PartitionSpec as P

RADIUS = 3
TAPS = 2 * RADIUS + 1
WINDOW = 2
REACH = 8
OFFS = 2 * REACH + 1
SIDE = 4
CHUNK = 256
LOW = CHUNK // 2
EDGE = 12
ROWS = 16
BAND = 2 * ROWS
PIECE = 256
FRAMES = SIDE * SIDE
KDIM = 640
MESH = pl.DeviceIdType.MESH
F32 = jnp.float32
BF16 = jnp.bfloat16


def iota(shape, axis):
    return lax.broadcasted_iota(jnp.int32, shape, axis)


def three(value):
    high = value.astype(BF16)
    rest = value - high.astype(F32)
    middle = rest.astype(BF16)
    low = (rest - middle.astype(F32)).astype(BF16)
    return jnp.concatenate([high, middle, low], axis=0)


def pick(value, table):
    rows = value.shape[0]
    out = jnp.dot(three(value), table, preferred_element_type=F32)
    return out[:rows] + out[rows : 2 * rows] + out[2 * rows :]


def left(value, amount):
    width = value.shape[1]
    return value if amount % width == 0 else pltpu.roll(value, (-amount) % width, 1)


def kernel(
    tiles, est, frames, shifts, blur, out,
    taps_in, xw, fr, zs, fb, sb, xs, px, pg, xb, aa, af, hh, d1, r1, d2, r2, pr, mine,
    load_sem, hsend, hrecv, fsend, frecv, ssend, srecv,
    e1send, e1recv, e2send, e2recv, gsend, grecv,
):
    t = lax.axis_index("tile")
    f = lax.axis_index("frame")
    x = f // SIDE
    y = f % SIDE
    c = SIDE * y + x
    last = FRAMES - 1
    at_low = (last - c) // last
    at_high = c // last
    start = pl.multiple_of(128 * (2 * c - 1 + at_low - at_high), 128)
    lane0 = pl.multiple_of(128 * (1 + at_low - at_high), 128)
    up = lax.rem(t + tiles - 1, tiles)
    down = lax.rem(t + 1, tiles)

    def ypeer(e):
        return {"frame": SIDE * x + lax.rem(y + e, SIDE)}

    def xpeer(e):
        return {"frame": SIDE * lax.rem(x + e, SIDE) + y}

    def remote(src, dst, send, recv, device):
        return pltpu.make_async_remote_copy(
            src_ref=src, dst_ref=dst, send_sem=send, recv_sem=recv, device_id=device, device_id_type=MESH
        )

    def across_tiles(above, below):
        has_above, has_below = t > 0, t < tiles - 1

        class Pair:
            def start(self):
                pl.when(has_above)(above.start)
                pl.when(has_below)(below.start)

            def wait_recv(self):
                pl.when(has_above)(below.wait_recv)
                pl.when(has_below)(above.wait_recv)

            def wait_send(self):
                pl.when(has_above)(above.wait_send)
                pl.when(has_below)(below.wait_send)

        return Pair()

    def peer(slot):
        px_, py_ = lax.rem(x + slot // SIDE, SIDE), lax.rem(y + slot % SIDE, SIDE)
        return {"frame": SIDE * px_ + py_}, SIDE * py_ + px_

    order = sorted(range(1, FRAMES), key=lambda slot: -(min(slot // SIDE, 4 - slot // SIDE) + 2 * min(slot % SIDE, 4 - slot % SIDE)))

    window = est.at[:, pl.ds(start, 512)]
    load_f = pltpu.make_async_copy(frames.at[0], fr, load_sem.at[0])
    load_x = pltpu.make_async_copy(window, xw.at[pl.ds(ROWS, ROWS), pl.ds(lane0, 512)], load_sem.at[1])
    load_s = pltpu.make_async_copy(shifts, sb.at[0], load_sem.at[2])
    load_b = pltpu.make_async_copy(blur, taps_in, load_sem.at[3])

    barrier = pltpu.get_barrier_semaphore()

    def greet(device):
        pl.semaphore_signal(barrier, inc=1, device_id=device, device_id_type=MESH)

    load_f.start()
    for slot in order:
        greet(peer(slot)[0])
    pl.when(t > 0)(lambda: greet({"tile": up}))
    pl.when(t < tiles - 1)(lambda: greet({"tile": down}))
    load_x.start()
    load_s.start()
    load_b.start()

    load_f.wait()
    lane = iota((8, 128), 1)
    before = jnp.zeros((8, 128), F32)
    for tile in range(FRAMES + 1):
        rolled = pltpu.roll(fr[:, 128 * tile : 128 * tile + 128], EDGE, 1) if tile < FRAMES else jnp.zeros((8, 128), F32)
        zs[:, 128 * tile : 128 * tile + 128] = jnp.where(lane < EDGE, before, rolled)
        before = rolled
    pl.semaphore_wait(barrier, FRAMES + (t + tiles - 1) // tiles - (t + 1) // tiles)

    started = []

    def go(copy):
        copy.start()
        started.append(copy)
        return copy

    fcopies = {}
    scopies = {}
    for slot in order:
        scopies[slot] = go(remote(shifts, sb.at[slot], ssend.at[slot], srecv.at[slot], peer(slot)[0]))
    halo = go(
        across_tiles(
            remote(window, xw.at[pl.ds(2 * ROWS, ROWS), pl.ds(lane0, 512)], hsend.at[0], hrecv.at[1], {"tile": up}),
            remote(window, xw.at[pl.ds(0, ROWS), pl.ds(lane0, 512)], hsend.at[1], hrecv.at[0], {"tile": down}),
        )
    )
    for slot in order:
        device, chunk = peer(slot)
        source = zs.at[:, pl.ds(pl.multiple_of(LOW * chunk, LOW), PIECE)]
        fcopies[slot] = go(remote(source, fb.at[slot], fsend.at[slot], frecv.at[slot], device))
    fb[0] = zs[:, pl.ds(pl.multiple_of(LOW * c, LOW), PIECE)]

    high_cols = CHUNK * FRAMES
    load_x.wait()
    halo.wait_recv()
    row = ROWS * t - ROWS + iota((3 * ROWS, 512), 0)
    col = CHUNK * c - 128 + iota((3 * ROWS, 512), 1)
    inside = (row >= 0) & (row < ROWS * tiles) & (col >= 0) & (col < high_cols)
    raw = jnp.where(inside, xw[:, 128:640], 0.0)
    lane_in = iota((512, 256), 0)
    lane_out = iota((512, 256), 1)
    for phase in range(2):
        table = jnp.where(lane_in == 96 + phase + 2 * lane_out, 1.0, 0.0).astype(BF16)
        xs[phase] = pick(raw, table)

    row = ROWS * t - ROWS + iota((3 * ROWS, 256), 0)
    col = CHUNK * c - 32 + 2 * iota((3 * ROWS, 256), 1)
    inside = (row >= 0) & (row < ROWS * tiles) & (col >= 0) & (col < high_cols)
    gain = jnp.where(inside, 2.0, 1.0)
    pg[0] = left(gain, -1)
    pg[1] = gain
    pg[2] = left(gain, 1)

    def stage_model(lo):
        for off in range(OFFS):
            xb[BAND * off : BAND * off + BAND] = left(xs[off % 2, lo : lo + BAND], off // 2)

    def stage_prior(lo, count):
        for phase in range(2):
            double = 2.0 * xs[phase, lo : lo + count]
            px[3 * phase, lo : lo + count] = left(double, -1)
            px[3 * phase + 1, lo : lo + count] = double
            px[3 * phase + 2, lo : lo + count] = left(double, 1)

    def prior(phase, lo, count):
        centre = px[3 * phase + 1, lo : lo + count]
        total = jnp.zeros((count, 256), F32)
        for side in range(-WINDOW, WINDOW + 1):
            other = (phase + side) % 2
            lanes = (phase + side - other) // 2 + 1
            for down_off in range(-WINDOW, WINDOW + 1):
                if down_off == 0 and side == 0:
                    continue
                rows = slice(lo + down_off, lo + down_off + count)
                weight = 0.7 ** (abs(down_off) + abs(side))
                slope = jnp.tanh(centre - px[3 * other + lanes, rows])
                total = total + (weight * slope) * pg[lanes, rows]
        return total

    xb[OFFS * BAND : KDIM] = jnp.zeros((KDIM - OFFS * BAND, 256), F32)
    aa[OFFS * BAND : KDIM] = jnp.zeros((KDIM - OFFS * BAND, 128), F32)
    stage_model(REACH)
    stage_prior(0, 3 * ROWS)

    for phase in range(2):
        pr[phase] = xs[phase, REACH : REACH + BAND] - 0.005 * prior(phase, REACH, BAND)

    load_s.wait()
    for copy in scopies.values():
        copy.wait_recv()
    frame = iota((1, 128), 1) // 8
    down_shift = jnp.zeros((1, 128), jnp.int32)
    side_shift = jnp.zeros((1, 128), jnp.int32)
    for slot in range(FRAMES):
        pair = sb[slot]
        down_shift = jnp.where(frame == slot, pair[0:1, 0:1], down_shift)
        side_shift = jnp.where(frame == slot, pair[0:1, 1:2], side_shift)
    load_b.wait()
    blur_sum = taps_in[0]
    for tap in range(1, TAPS):
        blur_sum = blur_sum + taps_in[tap]
    scale = jnp.full((1, 128), blur_sum)
    taps = [jnp.full((1, 128), taps_in[tap]) / scale for tap in range(TAPS)]

    def tap_at(distance):
        total = jnp.zeros(distance.shape, F32)
        for tap in range(TAPS):
            total = jnp.where(distance == tap - RADIUS, jnp.broadcast_to(taps[tap], distance.shape), total)
        return total

    place = iota((BAND, 128), 0) - REACH - 2 * (iota((BAND, 128), 1) % 8)
    by_row = tap_at(place - down_shift)
    by_col = tap_at(iota((24, 128), 0) - REACH - side_shift)
    for off in range(OFFS):
        aa[BAND * off : BAND * off + BAND] = by_row * by_col[off : off + 1]
    for block in range(KDIM // 128):
        af[:, 128 * block : 128 * block + 128] = aa[128 * block : 128 * block + 128].T

    low = LOW * c - EDGE + iota((128, 256), 1)
    live = (low >= 0) & (low < LOW * FRAMES)

    def misfits():
        pred = jnp.dot(af[...], xb[...], precision=lax.Precision.HIGH, preferred_element_type=F32)
        return pred

    def adjoint(pred):
        gap = jnp.where(live, jnp.tanh(pred - fb[...].reshape(128, PIECE)), 0.0)
        hh[...] = jnp.dot(
            aa[: OFFS * BAND], gap, precision=lax.Precision.HIGH, preferred_element_type=F32
        )

    pred = misfits()
    for copy in fcopies.values():
        copy.wait_recv()
    adjoint(pred)
    for phase in range(2):
        total = jnp.zeros((BAND, 256), F32)
        for off in range(phase, OFFS, 2):
            total = total + left(hh[BAND * off : BAND * off + BAND], -(off // 2))
        d1[phase] = total
    first = go(
        across_tiles(
            remote(d1.at[:, pl.ds(0, ROWS)], r1.at[:, pl.ds(ROWS, ROWS)], e1send.at[0], e1recv.at[1], {"tile": up}),
            remote(d1.at[:, pl.ds(ROWS, ROWS)], r1.at[:, pl.ds(0, ROWS)], e1send.at[1], e1recv.at[0], {"tile": down}),
        )
    )
    reach_row = ROWS * t - REACH + iota((BAND, 256), 0)
    edge_row = (reach_row < REACH) | (reach_row >= ROWS * tiles - REACH)
    within = pg[1, REACH : REACH + BAND] > 1.5
    first.wait_recv()
    for phase in range(2):
        theirs = jnp.where(edge_row, 0.0, r1[phase])
        xs[phase, REACH : REACH + BAND] = jnp.where(within, pr[phase] - 0.1 * (d1[phase] + theirs), 0.0)

    stage_model(REACH)
    adjoint(misfits())
    both = []
    for phase in range(2):
        total = jnp.zeros((BAND, 128), F32)
        for off in range(phase, OFFS, 2):
            total = total + left(hh[BAND * off : BAND * off + BAND], ROWS - off // 2)[:, :128]
        d2[0, phase] = total[:REACH]
        d2[1, phase] = total[3 * REACH :]
        both.append(total[REACH : 3 * REACH])
    second = go(
        across_tiles(
            remote(d2.at[0], r2.at[1], e2send.at[0], e2recv.at[1], {"tile": up}),
            remote(d2.at[1], r2.at[0], e2send.at[1], e2recv.at[0], {"tile": down}),
        )
    )

    stage_prior(REACH, BAND)
    for phase in range(2):
        kept = xs[phase, ROWS : 2 * ROWS] - 0.005 * prior(phase, ROWS, ROWS)
        both[phase] = left(kept, ROWS)[:, :128] - 0.1 * both[phase]
    lane_in = iota((CHUNK, CHUNK), 0)
    lane_out = iota((CHUNK, CHUNK), 1)
    table = jnp.where(lane_out == jnp.where(lane_in < LOW, 2 * lane_in, 2 * lane_in - CHUNK + 1), 1.0, 0.0).astype(BF16)
    own_row = ROWS * t + iota((ROWS, LOW), 0)
    edge_row = (own_row < REACH) | (own_row >= ROWS * tiles - REACH)
    second.wait_recv()
    halves = []
    for phase in range(2):
        theirs = jnp.concatenate([r2[0, phase], r2[1, phase]], axis=0)
        halves.append(both[phase] - 0.1 * jnp.where(edge_row, 0.0, theirs))
    result = pick(jnp.concatenate(halves, axis=1), table)

    def chunk_of(ey):
        source = SIDE * lax.rem(y + SIDE - ey, SIDE) + x
        return out.at[:, pl.ds(pl.multiple_of(CHUNK * source, CHUNK), CHUNK)]

    mine[...] = result
    keep = pltpu.make_async_copy(mine, chunk_of(0), load_sem.at[4])
    gathers = {}
    for e in (2, 1, 3):
        gathers[e] = go(remote(mine, chunk_of(0), gsend.at[e], grecv.at[e], ypeer(e)))

    def spread(ey):
        source = chunk_of(ey) if ey else mine
        for ex in (2, 1, 3):
            slot = SIDE * ex + ey
            gathers[slot] = go(remote(source, chunk_of(ey), gsend.at[slot], grecv.at[slot], xpeer(ex)))

    spread(0)
    keep.start()
    for ey in (1, 3, 2):
        gathers[ey].wait_recv()
        spread(ey)
    for slot, copy in gathers.items():
        if slot >= SIDE:
            copy.wait_recv()
    keep.wait()
    for copy in started:
        copy.wait_send()


def local(tiles, estimate, frames, shifts, blur):
    vmem = lambda *shape: pltpu.VMEM(shape, F32)
    dma = lambda n: pltpu.SemaphoreType.DMA((n,))
    return pl.pallas_call(
        functools.partial(kernel, tiles),
        out_shape=jax.ShapeDtypeStruct(estimate.shape, F32),
        in_specs=[pl.BlockSpec(memory_space=pltpu.HBM)] * 4,
        out_specs=pl.BlockSpec(memory_space=pl.ANY),
        scratch_shapes=[
            pltpu.SMEM((TAPS,), F32),
            vmem(3 * ROWS, 768),
            vmem(8, FRAMES * LOW),
            vmem(8, FRAMES * LOW + 128),
            vmem(FRAMES, 8, PIECE),
            pltpu.VMEM((FRAMES, 1, 2), jnp.int32),
            vmem(2, 3 * ROWS, 256),
            vmem(6, 3 * ROWS, 256),
            vmem(3, 3 * ROWS, 256),
            vmem(KDIM, 256),
            vmem(KDIM, 128),
            vmem(128, KDIM),
            vmem(OFFS * BAND, 256),
            vmem(2, BAND, 256),
            vmem(2, BAND, 256),
            vmem(2, 2, REACH, 128),
            vmem(2, 2, REACH, 128),
            vmem(2, BAND, 256),
            vmem(ROWS, CHUNK),
            dma(5), dma(2), dma(2), dma(FRAMES), dma(FRAMES), dma(FRAMES), dma(FRAMES),
            dma(2), dma(2), dma(2), dma(2), dma(FRAMES), dma(FRAMES),
        ],
        compiler_params=pltpu.CompilerParams(collective_id=0, has_side_effects=True, vmem_limit_bytes=16 * 1024 * 1024),
    )(*(pltpu.with_memory_space_constraint(value, pltpu.HBM) for value in (estimate, frames, shifts, blur)))


def solution(mesh):
    placed = (P("tile", None), P("frame", "tile", None), P("frame", None), P())
    return jax.shard_map(
        functools.partial(local, mesh.shape["tile"]),
        mesh=mesh, in_specs=placed, out_specs=P("tile", None), check_vma=False,
    )
```

```python
import functools

import jax
import jax.numpy as jnp
from jax import lax
from jax.experimental import pallas as pl
from jax.experimental.pallas import tpu as pltpu
from jax.sharding import PartitionSpec as P

RADIUS = 3
TAPS = 2 * RADIUS + 1
WINDOW = 2
REACH = 8
OFFS = 2 * REACH + 1
SIDE = 4
CHUNK = 256
LOW = CHUNK // 2
EDGE = 12
ROWS = 16
BAND = 2 * ROWS
PIECE = 256
FRAMES = SIDE * SIDE
KDIM = 640
MESH = pl.DeviceIdType.MESH
F32 = jnp.float32
BF16 = jnp.bfloat16


def iota(shape, axis):
    return lax.broadcasted_iota(jnp.int32, shape, axis)


def three(value):
    high = value.astype(BF16)
    rest = value - high.astype(F32)
    middle = rest.astype(BF16)
    low = (rest - middle.astype(F32)).astype(BF16)
    return jnp.concatenate([high, middle, low], axis=0)


def pick(value, table):
    rows = value.shape[0]
    out = jnp.dot(three(value), table, preferred_element_type=F32)
    return out[:rows] + out[rows : 2 * rows] + out[2 * rows :]


def left(value, amount):
    width = value.shape[1]
    return value if amount % width == 0 else pltpu.roll(value, (-amount) % width, 1)


def kernel(
    tiles, est, frames, shifts, blur, out,
    taps_in, xw, fr, zs, fb, sb, xs, px, pg, xb, aa, af, hh, d1, r1, d2, r2, pr, mine,
    load_sem, hsend, hrecv, fsend, frecv, ssend, srecv,
    e1send, e1recv, e2send, e2recv, gsend, grecv,
):
    t = lax.axis_index("tile")
    f = lax.axis_index("frame")
    x = f // SIDE
    y = f % SIDE
    c = SIDE * y + x
    last = FRAMES - 1
    at_low = (last - c) // last
    at_high = c // last
    start = pl.multiple_of(128 * (2 * c - 1 + at_low - at_high), 128)
    lane0 = pl.multiple_of(128 * (1 + at_low - at_high), 128)
    up = lax.rem(t + tiles - 1, tiles)
    down = lax.rem(t + 1, tiles)

    def remote(src, dst, send, recv, device):
        return pltpu.make_async_remote_copy(
            src_ref=src, dst_ref=dst, send_sem=send, recv_sem=recv, device_id=device, device_id_type=MESH
        )

    def across_tiles(above, below):
        has_above, has_below = t > 0, t < tiles - 1

        class Pair:
            def start(self):
                pl.when(has_above)(above.start)
                pl.when(has_below)(below.start)

            def wait_recv(self):
                pl.when(has_above)(below.wait_recv)
                pl.when(has_below)(above.wait_recv)

            def wait_send(self):
                pl.when(has_above)(above.wait_send)
                pl.when(has_below)(below.wait_send)

        return Pair()

    def peer(slot):
        px_, py_ = lax.rem(x + slot // SIDE, SIDE), lax.rem(y + slot % SIDE, SIDE)
        return {"frame": SIDE * px_ + py_}, SIDE * py_ + px_

    order = sorted(range(1, FRAMES), key=lambda slot: -(min(slot // SIDE, 4 - slot // SIDE) + 2 * min(slot % SIDE, 4 - slot % SIDE)))

    window = est.at[:, pl.ds(start, 512)]
    load_f = pltpu.make_async_copy(frames.at[0], fr, load_sem.at[0])
    load_x = pltpu.make_async_copy(window, xw.at[pl.ds(ROWS, ROWS), pl.ds(lane0, 512)], load_sem.at[1])
    load_s = pltpu.make_async_copy(shifts, sb.at[0], load_sem.at[2])
    load_b = pltpu.make_async_copy(blur, taps_in, load_sem.at[3])

    barrier = pltpu.get_barrier_semaphore()

    def greet(device):
        pl.semaphore_signal(barrier, inc=1, device_id=device, device_id_type=MESH)

    load_f.start()
    for slot in order:
        greet(peer(slot)[0])
    pl.when(t > 0)(lambda: greet({"tile": up}))
    pl.when(t < tiles - 1)(lambda: greet({"tile": down}))
    load_x.start()
    load_s.start()
    load_b.start()

    load_f.wait()
    lane = iota((8, 128), 1)
    before = jnp.zeros((8, 128), F32)
    for tile in range(FRAMES + 1):
        rolled = pltpu.roll(fr[:, 128 * tile : 128 * tile + 128], EDGE, 1) if tile < FRAMES else jnp.zeros((8, 128), F32)
        zs[:, 128 * tile : 128 * tile + 128] = jnp.where(lane < EDGE, before, rolled)
        before = rolled
    pl.semaphore_wait(barrier, FRAMES + (t + tiles - 1) // tiles - (t + 1) // tiles)

    started = []

    def go(copy):
        copy.start()
        started.append(copy)
        return copy

    fcopies = {}
    scopies = {}
    for slot in order:
        scopies[slot] = go(remote(shifts, sb.at[slot], ssend.at[slot], srecv.at[slot], peer(slot)[0]))
    halo = go(
        across_tiles(
            remote(window, xw.at[pl.ds(2 * ROWS, ROWS), pl.ds(lane0, 512)], hsend.at[0], hrecv.at[1], {"tile": up}),
            remote(window, xw.at[pl.ds(0, ROWS), pl.ds(lane0, 512)], hsend.at[1], hrecv.at[0], {"tile": down}),
        )
    )
    for slot in order:
        device, chunk = peer(slot)
        source = zs.at[:, pl.ds(pl.multiple_of(LOW * chunk, LOW), PIECE)]
        fcopies[slot] = go(remote(source, fb.at[slot], fsend.at[slot], frecv.at[slot], device))
    fb[0] = zs[:, pl.ds(pl.multiple_of(LOW * c, LOW), PIECE)]

    high_cols = CHUNK * FRAMES
    load_x.wait()
    halo.wait_recv()
    row = ROWS * t - ROWS + iota((3 * ROWS, 512), 0)
    col = CHUNK * c - 128 + iota((3 * ROWS, 512), 1)
    inside = (row >= 0) & (row < ROWS * tiles) & (col >= 0) & (col < high_cols)
    raw = jnp.where(inside, xw[:, 128:640], 0.0)
    lane_in = iota((512, 256), 0)
    lane_out = iota((512, 256), 1)
    for phase in range(2):
        table = jnp.where(lane_in == 96 + phase + 2 * lane_out, 1.0, 0.0).astype(BF16)
        xs[phase] = pick(raw, table)

    row = ROWS * t - ROWS + iota((3 * ROWS, 256), 0)
    col = CHUNK * c - 32 + 2 * iota((3 * ROWS, 256), 1)
    inside = (row >= 0) & (row < ROWS * tiles) & (col >= 0) & (col < high_cols)
    gain = jnp.where(inside, 2.0, 1.0)
    pg[0] = left(gain, -1)
    pg[1] = gain
    pg[2] = left(gain, 1)

    def stage_model(lo):
        for off in range(OFFS):
            xb[BAND * off : BAND * off + BAND] = left(xs[off % 2, lo : lo + BAND], off // 2)

    def stage_prior(lo, count):
        for phase in range(2):
            double = 2.0 * xs[phase, lo : lo + count]
            px[3 * phase, lo : lo + count] = left(double, -1)
            px[3 * phase + 1, lo : lo + count] = double
            px[3 * phase + 2, lo : lo + count] = left(double, 1)

    def prior(phase, lo, count):
        centre = px[3 * phase + 1, lo : lo + count]
        total = jnp.zeros((count, 256), F32)
        for side in range(-WINDOW, WINDOW + 1):
            other = (phase + side) % 2
            lanes = (phase + side - other) // 2 + 1
            for down_off in range(-WINDOW, WINDOW + 1):
                if down_off == 0 and side == 0:
                    continue
                rows = slice(lo + down_off, lo + down_off + count)
                weight = 0.7 ** (abs(down_off) + abs(side))
                slope = jnp.tanh(centre - px[3 * other + lanes, rows])
                total = total + (weight * slope) * pg[lanes, rows]
        return total

    xb[OFFS * BAND : KDIM] = jnp.zeros((KDIM - OFFS * BAND, 256), F32)
    aa[OFFS * BAND : KDIM] = jnp.zeros((KDIM - OFFS * BAND, 128), F32)
    stage_model(REACH)
    stage_prior(0, 3 * ROWS)

    for phase in range(2):
        pr[phase] = xs[phase, REACH : REACH + BAND] - 0.005 * prior(phase, REACH, BAND)

    load_s.wait()
    for copy in scopies.values():
        copy.wait_recv()
    frame = iota((1, 128), 1) // 8
    down_shift = jnp.zeros((1, 128), jnp.int32)
    side_shift = jnp.zeros((1, 128), jnp.int32)
    for slot in range(FRAMES):
        pair = sb[slot]
        down_shift = jnp.where(frame == slot, pair[0:1, 0:1], down_shift)
        side_shift = jnp.where(frame == slot, pair[0:1, 1:2], side_shift)
    load_b.wait()
    blur_sum = taps_in[0]
    for tap in range(1, TAPS):
        blur_sum = blur_sum + taps_in[tap]
    scale = jnp.full((1, 128), blur_sum)
    taps = [jnp.full((1, 128), taps_in[tap]) / scale for tap in range(TAPS)]

    def tap_at(distance):
        total = jnp.zeros(distance.shape, F32)
        for tap in range(TAPS):
            total = jnp.where(distance == tap - RADIUS, jnp.broadcast_to(taps[tap], distance.shape), total)
        return total

    place = iota((BAND, 128), 0) - REACH - 2 * (iota((BAND, 128), 1) % 8)
    by_row = tap_at(place - down_shift)
    by_col = tap_at(iota((24, 128), 0) - REACH - side_shift)
    for off in range(OFFS):
        aa[BAND * off : BAND * off + BAND] = by_row * by_col[off : off + 1]
    for block in range(KDIM // 128):
        af[:, 128 * block : 128 * block + 128] = aa[128 * block : 128 * block + 128].T

    low = LOW * c - EDGE + iota((128, 256), 1)
    live = (low >= 0) & (low < LOW * FRAMES)

    def misfits():
        pred = jnp.dot(af[...], xb[...], precision=lax.Precision.HIGH, preferred_element_type=F32)
        return pred

    def adjoint(pred):
        gap = jnp.where(live, jnp.tanh(pred - fb[...].reshape(128, PIECE)), 0.0)
        hh[...] = jnp.dot(
            aa[: OFFS * BAND], gap, precision=lax.Precision.HIGH, preferred_element_type=F32
        )

    pred = misfits()
    for copy in fcopies.values():
        copy.wait_recv()
    adjoint(pred)
    for phase in range(2):
        total = jnp.zeros((BAND, 256), F32)
        for off in range(phase, OFFS, 2):
            total = total + left(hh[BAND * off : BAND * off + BAND], -(off // 2))
        d1[phase] = total
    first = go(
        across_tiles(
            remote(d1.at[:, pl.ds(0, ROWS)], r1.at[:, pl.ds(ROWS, ROWS)], e1send.at[0], e1recv.at[1], {"tile": up}),
            remote(d1.at[:, pl.ds(ROWS, ROWS)], r1.at[:, pl.ds(0, ROWS)], e1send.at[1], e1recv.at[0], {"tile": down}),
        )
    )
    reach_row = ROWS * t - REACH + iota((BAND, 256), 0)
    edge_row = (reach_row < REACH) | (reach_row >= ROWS * tiles - REACH)
    within = pg[1, REACH : REACH + BAND] > 1.5
    first.wait_recv()
    for phase in range(2):
        theirs = jnp.where(edge_row, 0.0, r1[phase])
        xs[phase, REACH : REACH + BAND] = jnp.where(within, pr[phase] - 0.1 * (d1[phase] + theirs), 0.0)

    stage_model(REACH)
    adjoint(misfits())
    both = []
    for phase in range(2):
        total = jnp.zeros((BAND, 128), F32)
        for off in range(phase, OFFS, 2):
            total = total + left(hh[BAND * off : BAND * off + BAND], ROWS - off // 2)[:, :128]
        d2[0, phase] = total[:REACH]
        d2[1, phase] = total[3 * REACH :]
        both.append(total[REACH : 3 * REACH])
    second = go(
        across_tiles(
            remote(d2.at[0], r2.at[1], e2send.at[0], e2recv.at[1], {"tile": up}),
            remote(d2.at[1], r2.at[0], e2send.at[1], e2recv.at[0], {"tile": down}),
        )
    )

    stage_prior(REACH, BAND)
    for phase in range(2):
        kept = xs[phase, ROWS : 2 * ROWS] - 0.005 * prior(phase, ROWS, ROWS)
        both[phase] = left(kept, ROWS)[:, :128] - 0.1 * both[phase]
    lane_in = iota((CHUNK, CHUNK), 0)
    lane_out = iota((CHUNK, CHUNK), 1)
    table = jnp.where(lane_out == jnp.where(lane_in < LOW, 2 * lane_in, 2 * lane_in - CHUNK + 1), 1.0, 0.0).astype(BF16)
    own_row = ROWS * t + iota((ROWS, LOW), 0)
    edge_row = (own_row < REACH) | (own_row >= ROWS * tiles - REACH)
    second.wait_recv()
    halves = []
    for phase in range(2):
        theirs = jnp.concatenate([r2[0, phase], r2[1, phase]], axis=0)
        halves.append(both[phase] - 0.1 * jnp.where(edge_row, 0.0, theirs))
    result = pick(jnp.concatenate(halves, axis=1), table)

    mine[...] = result
    own = out.at[:, pl.ds(pl.multiple_of(CHUNK * c, CHUNK), CHUNK)]
    keep = pltpu.make_async_copy(mine, own, load_sem.at[4])
    gathers = {slot: go(remote(mine, own, gsend.at[slot], grecv.at[slot], peer(slot)[0])) for slot in order}
    keep.start()
    for copy in gathers.values():
        copy.wait_recv()
    keep.wait()
    for copy in started:
        copy.wait_send()


def local(tiles, estimate, frames, shifts, blur):
    vmem = lambda *shape: pltpu.VMEM(shape, F32)
    dma = lambda n: pltpu.SemaphoreType.DMA((n,))
    return pl.pallas_call(
        functools.partial(kernel, tiles),
        out_shape=jax.ShapeDtypeStruct(estimate.shape, F32),
        in_specs=[pl.BlockSpec(memory_space=pltpu.HBM)] * 4,
        out_specs=pl.BlockSpec(memory_space=pl.ANY),
        scratch_shapes=[
            pltpu.SMEM((TAPS,), F32),
            vmem(3 * ROWS, 768),
            vmem(8, FRAMES * LOW),
            vmem(8, FRAMES * LOW + 128),
            vmem(FRAMES, 8, PIECE),
            pltpu.VMEM((FRAMES, 1, 2), jnp.int32),
            vmem(2, 3 * ROWS, 256),
            vmem(6, 3 * ROWS, 256),
            vmem(3, 3 * ROWS, 256),
            vmem(KDIM, 256),
            vmem(KDIM, 128),
            vmem(128, KDIM),
            vmem(OFFS * BAND, 256),
            vmem(2, BAND, 256),
            vmem(2, BAND, 256),
            vmem(2, 2, REACH, 128),
            vmem(2, 2, REACH, 128),
            vmem(2, BAND, 256),
            vmem(ROWS, CHUNK),
            dma(5), dma(2), dma(2), dma(FRAMES), dma(FRAMES), dma(FRAMES), dma(FRAMES),
            dma(2), dma(2), dma(2), dma(2), dma(FRAMES), dma(FRAMES),
        ],
        compiler_params=pltpu.CompilerParams(collective_id=0, has_side_effects=True, vmem_limit_bytes=16 * 1024 * 1024),
    )(*(pltpu.with_memory_space_constraint(value, pltpu.HBM) for value in (estimate, frames, shifts, blur)))


def solution(mesh):
    placed = (P("tile", None), P("frame", "tile", None), P("frame", None), P())
    return jax.shard_map(
        functools.partial(local, mesh.shape["tile"]),
        mesh=mesh, in_specs=placed, out_specs=P("tile", None), check_vma=False,
    )
```

```python
import functools

import jax
import jax.numpy as jnp
from jax import lax
from jax.experimental import pallas as pl
from jax.experimental.pallas import tpu as pltpu
from jax.sharding import PartitionSpec as P

RADIUS = 3
TAPS = 2 * RADIUS + 1
WINDOW = 2
REACH = 8
OFFS = 2 * REACH + 1
SIDE = 4
CHUNK = 256
LOW = CHUNK // 2
EDGE = 12
ROWS = 16
BAND = 2 * ROWS
SLOT = 32
FRAMES = SIDE * SIDE
KDIM = 640
MESH = pl.DeviceIdType.MESH
F32 = jnp.float32
BF16 = jnp.bfloat16


def iota(shape, axis):
    return lax.broadcasted_iota(jnp.int32, shape, axis)


def three(value):
    high = value.astype(BF16)
    rest = value - high.astype(F32)
    middle = rest.astype(BF16)
    low = (rest - middle.astype(F32)).astype(BF16)
    return jnp.concatenate([high, middle, low], axis=0)


def pick(value, table):
    rows = value.shape[0]
    out = jnp.dot(three(value), table, preferred_element_type=F32)
    return out[:rows] + out[rows : 2 * rows] + out[2 * rows :]


def left(value, amount):
    width = value.shape[1]
    return value if amount % width == 0 else pltpu.roll(value, (-amount) % width, 1)


def kernel(
    tiles, est, frames, shifts, blur, out,
    taps_in, shift_in, xw, fr, zs, zp, fb, hp, fh, xs, px, pg, xh, xl, aa, a3, af, hh, d1, r1, d2, r2, pr, mine,
    load_sem, hsend, hrecv, fsend, frecv, ssend, srecv,
    e1send, e1recv, e2send, e2recv, gsend, grecv,
):
    t = lax.axis_index("tile")
    f = lax.axis_index("frame")
    x = f // SIDE
    y = f % SIDE
    c = SIDE * y + x
    last = FRAMES - 1
    at_low = (last - c) // last
    at_high = c // last
    start = pl.multiple_of(128 * (2 * c - 1 + at_low - at_high), 128)
    lane0 = pl.multiple_of(128 * (1 + at_low - at_high), 128)
    up = lax.rem(t + tiles - 1, tiles)
    down = lax.rem(t + 1, tiles)

    def remote(src, dst, send, recv, device):
        return pltpu.make_async_remote_copy(
            src_ref=src, dst_ref=dst, send_sem=send, recv_sem=recv, device_id=device, device_id_type=MESH
        )

    def across_tiles(above, below):
        has_above, has_below = t > 0, t < tiles - 1

        class Pair:
            def start(self):
                pl.when(has_above)(above.start)
                pl.when(has_below)(below.start)

            def wait_recv(self):
                pl.when(has_above)(below.wait_recv)
                pl.when(has_below)(above.wait_recv)

            def wait_send(self):
                pl.when(has_above)(above.wait_send)
                pl.when(has_below)(below.wait_send)

        return Pair()

    def peer(slot):
        px_, py_ = lax.rem(x + slot // SIDE, SIDE), lax.rem(y + slot % SIDE, SIDE)
        return {"frame": SIDE * px_ + py_}, SIDE * py_ + px_

    order = sorted(range(1, FRAMES), key=lambda slot: -(min(slot // SIDE, 4 - slot // SIDE) + 2 * min(slot % SIDE, 4 - slot % SIDE)))

    window = est.at[:, pl.ds(start, 512)]
    load_f = pltpu.make_async_copy(frames.at[0], fr, load_sem.at[0])
    load_x = pltpu.make_async_copy(window, xw.at[pl.ds(ROWS, ROWS), pl.ds(lane0, 512)], load_sem.at[1])
    load_s = pltpu.make_async_copy(shifts, shift_in, load_sem.at[2])
    load_b = pltpu.make_async_copy(blur, taps_in, load_sem.at[3])

    barrier = pltpu.get_barrier_semaphore()

    def greet(device):
        pl.semaphore_signal(barrier, inc=1, device_id=device, device_id_type=MESH)

    load_f.start()
    load_s.start()
    for slot in order:
        greet(peer(slot)[0])
    pl.when(t > 0)(lambda: greet({"tile": up}))
    pl.when(t < tiles - 1)(lambda: greet({"tile": down}))
    load_x.start()
    load_b.start()

    load_f.wait()
    lane = iota((8, 128), 1)
    sub = iota((8, 128), 0)
    before = jnp.zeros((8, 128), F32)
    load_s.wait()
    tail = jnp.where(
        lane == 2 * EDGE, jnp.full((8, 128), shift_in[0, 0].astype(F32)), jnp.full((8, 128), shift_in[0, 1].astype(F32))
    )
    for tile in range(FRAMES + 1):
        rolled = pltpu.roll(fr[:, 128 * tile : 128 * tile + 128], EDGE, 1) if tile < FRAMES else jnp.zeros((8, 128), F32)
        zs[:, 128 * tile : 128 * tile + 128] = jnp.where(lane < EDGE, before, rolled)
        before = rolled
        if tile:
            part = jnp.where(lane < 2 * EDGE, zs[:, 128 * tile : 128 * tile + 128], tail)
            part = jnp.where(lane < SLOT, part, 0.0)
            for turn in range(1, 4):
                part = jnp.where(sub % 4 == turn, pltpu.roll(part, 128 - SLOT * turn, 1), part)
            zp[tile - 1, 0:1] = jnp.sum(jnp.where(sub < 4, part, 0.0), axis=0, keepdims=True)
            zp[tile - 1, 1:2] = jnp.sum(jnp.where(sub < 4, 0.0, part), axis=0, keepdims=True)
    pl.semaphore_wait(barrier, FRAMES + (t + tiles - 1) // tiles - (t + 1) // tiles)

    started = []

    def go(copy):
        copy.start()
        started.append(copy)
        return copy

    fcopies = {}
    scopies = {}
    for slot in order:
        device, chunk = peer(slot)
        scopies[slot] = go(remote(zp.at[chunk], hp.at[slot], ssend.at[slot], srecv.at[slot], device))
    halo = go(
        across_tiles(
            remote(window, xw.at[pl.ds(2 * ROWS, ROWS), pl.ds(lane0, 512)], hsend.at[0], hrecv.at[1], {"tile": up}),
            remote(window, xw.at[pl.ds(0, ROWS), pl.ds(lane0, 512)], hsend.at[1], hrecv.at[0], {"tile": down}),
        )
    )
    for slot in order:
        device, chunk = peer(slot)
        source = zs.at[:, pl.ds(pl.multiple_of(LOW * chunk, LOW), LOW)]
        fcopies[slot] = go(remote(source, fb.at[slot], fsend.at[slot], frecv.at[slot], device))
    fb[0] = zs[:, pl.ds(pl.multiple_of(LOW * c, LOW), LOW)]
    hp[0] = zp[c]

    high_cols = CHUNK * FRAMES
    load_x.wait()
    halo.wait_recv()
    row = ROWS * t - ROWS + iota((3 * ROWS, 512), 0)
    col = CHUNK * c - 128 + iota((3 * ROWS, 512), 1)
    inside = (row >= 0) & (row < ROWS * tiles) & (col >= 0) & (col < high_cols)
    raw = jnp.where(inside, xw[:, 128:640], 0.0)
    lane_in = iota((512, 256), 0)
    lane_out = iota((512, 256), 1)
    for phase in range(2):
        table = jnp.where(lane_in == 96 + phase + 2 * lane_out, 1.0, 0.0).astype(BF16)
        xs[phase] = pick(raw, table)

    row = ROWS * t - ROWS + iota((3 * ROWS, 256), 0)
    col = CHUNK * c - 32 + 2 * iota((3 * ROWS, 256), 1)
    inside = (row >= 0) & (row < ROWS * tiles) & (col >= 0) & (col < high_cols)
    gain = jnp.where(inside, 2.0, 1.0)
    pg[0] = left(gain, -1)
    pg[1] = gain
    pg[2] = left(gain, 1)

    def split(value):
        high = value.astype(BF16)
        return high, (value - high.astype(F32)).astype(BF16)

    def stage_model(lo):
        for off in range(OFFS):
            rows = slice(BAND * off, BAND * off + BAND)
            xh[rows], xl[rows] = split(left(xs[off % 2, lo : lo + BAND], off // 2))

    def stage_prior(lo, count):
        for phase in range(2):
            double = 2.0 * xs[phase, lo : lo + count]
            px[3 * phase, lo : lo + count] = left(double, -1)
            px[3 * phase + 1, lo : lo + count] = double
            px[3 * phase + 2, lo : lo + count] = left(double, 1)

    def prior(phase, lo, count):
        centre = px[3 * phase + 1, lo : lo + count]
        total = jnp.zeros((count, 256), F32)
        for side in range(-WINDOW, WINDOW + 1):
            other = (phase + side) % 2
            lanes = (phase + side - other) // 2 + 1
            for down_off in range(-WINDOW, WINDOW + 1):
                if down_off == 0 and side == 0:
                    continue
                rows = slice(lo + down_off, lo + down_off + count)
                weight = 0.7 ** (abs(down_off) + abs(side))
                slope = jnp.tanh(centre - px[3 * other + lanes, rows])
                total = total + (weight * slope) * pg[lanes, rows]
        return total

    xh[OFFS * BAND : KDIM] = jnp.zeros((KDIM - OFFS * BAND, 256), BF16)
    xl[OFFS * BAND : KDIM] = jnp.zeros((KDIM - OFFS * BAND, 256), BF16)
    aa[OFFS * BAND : KDIM] = jnp.zeros((KDIM - OFFS * BAND, 128), F32)
    stage_model(REACH)
    stage_prior(0, 3 * ROWS)

    for phase in range(2):
        pr[phase] = xs[phase, REACH : REACH + BAND] - 0.005 * prior(phase, REACH, BAND)

    for copy in scopies.values():
        copy.wait_recv()
    frame = iota((1, 128), 1) // 8
    down_shift = jnp.zeros((1, 128), F32)
    side_shift = jnp.zeros((1, 128), F32)
    for slot in range(FRAMES):
        down_shift = jnp.where(frame == slot, hp[slot, 0:1, 2 * EDGE : 2 * EDGE + 1], down_shift)
        side_shift = jnp.where(frame == slot, hp[slot, 0:1, 2 * EDGE + 1 : 2 * EDGE + 2], side_shift)
        rows = jnp.where(
            sub < 4, jnp.broadcast_to(hp[slot, 0:1], (8, 128)), jnp.broadcast_to(hp[slot, 1:2], (8, 128))
        )
        for _ in range(2):
            rows = pltpu.roll(rows, 0, 1, stride=SLOT // 2, stride_axis=0)
        fh[8 * slot : 8 * slot + 8] = rows
    load_b.wait()
    blur_sum = taps_in[0]
    for tap in range(1, TAPS):
        blur_sum = blur_sum + taps_in[tap]
    scale = jnp.full((1, 128), blur_sum)
    taps = [jnp.full((1, 128), taps_in[tap]) / scale for tap in range(TAPS)]

    def tap_at(distance):
        total = jnp.zeros(distance.shape, F32)
        for tap in range(TAPS):
            total = jnp.where(distance == float(tap - RADIUS), jnp.broadcast_to(taps[tap], distance.shape), total)
        return total

    place = (iota((BAND, 128), 0) - REACH - 2 * (iota((BAND, 128), 1) % 8)).astype(F32)
    by_row = tap_at(place - down_shift)
    by_col = tap_at((iota((24, 128), 0) - REACH).astype(F32) - side_shift)
    for off in range(OFFS):
        rows = slice(BAND * off, BAND * off + BAND)
        entry = by_row * by_col[off : off + 1]
        aa[rows] = entry
        a3[rows, 0:128], a3[rows, 128:256] = split(entry)
        a3[rows, 256:384] = a3[rows, 0:128]
    for block in range(KDIM // 128):
        columns = slice(128 * block, 128 * block + 128)
        af[:128, columns], af[128:, columns] = split(aa[128 * block : 128 * block + 128].T)

    low = LOW * c - EDGE + iota((128, 256), 1)
    live = (low >= 0) & (low < LOW * FRAMES)

    def misfits():
        both = jnp.dot(af[...], xh[...], preferred_element_type=F32)
        return both[:128] + both[128:] + jnp.dot(af[:128], xl[...], preferred_element_type=F32)

    def adjoint(pred):
        seen = jnp.concatenate([fb[...].reshape(128, LOW), fh[...]], axis=1)
        high, rest = split(jnp.where(live, jnp.tanh(pred - seen), 0.0))
        hh[...] = jnp.dot(a3[...], jnp.concatenate([high, high, rest], axis=0), preferred_element_type=F32)

    pred = misfits()
    for copy in fcopies.values():
        copy.wait_recv()
    adjoint(pred)
    for phase in range(2):
        total = jnp.zeros((BAND, 256), F32)
        for off in range(phase, OFFS, 2):
            total = total + left(hh[BAND * off : BAND * off + BAND], -(off // 2))
        d1[phase] = total
    first = go(
        across_tiles(
            remote(d1.at[:, pl.ds(0, ROWS)], r1.at[:, pl.ds(ROWS, ROWS)], e1send.at[0], e1recv.at[1], {"tile": up}),
            remote(d1.at[:, pl.ds(ROWS, ROWS)], r1.at[:, pl.ds(0, ROWS)], e1send.at[1], e1recv.at[0], {"tile": down}),
        )
    )
    reach_row = ROWS * t - REACH + iota((BAND, 256), 0)
    edge_row = (reach_row < REACH) | (reach_row >= ROWS * tiles - REACH)
    within = pg[1, REACH : REACH + BAND] > 1.5
    first.wait_recv()
    for phase in range(2):
        theirs = jnp.where(edge_row, 0.0, r1[phase])
        xs[phase, REACH : REACH + BAND] = jnp.where(within, pr[phase] - 0.1 * (d1[phase] + theirs), 0.0)

    stage_model(REACH)
    adjoint(misfits())
    both = []
    for phase in range(2):
        total = jnp.zeros((BAND, 128), F32)
        for off in range(phase, OFFS, 2):
            total = total + left(hh[BAND * off : BAND * off + BAND], ROWS - off // 2)[:, :128]
        d2[0, phase] = total[:REACH]
        d2[1, phase] = total[3 * REACH :]
        both.append(total[REACH : 3 * REACH])
    second = go(
        across_tiles(
            remote(d2.at[0], r2.at[1], e2send.at[0], e2recv.at[1], {"tile": up}),
            remote(d2.at[1], r2.at[0], e2send.at[1], e2recv.at[0], {"tile": down}),
        )
    )

    stage_prior(REACH, BAND)
    for phase in range(2):
        kept = xs[phase, ROWS : 2 * ROWS] - 0.005 * prior(phase, ROWS, ROWS)
        both[phase] = left(kept, ROWS)[:, :128] - 0.1 * both[phase]
    lane_in = iota((CHUNK, CHUNK), 0)
    lane_out = iota((CHUNK, CHUNK), 1)
    table = jnp.where(lane_out == jnp.where(lane_in < LOW, 2 * lane_in, 2 * lane_in - CHUNK + 1), 1.0, 0.0).astype(BF16)
    own_row = ROWS * t + iota((ROWS, LOW), 0)
    edge_row = (own_row < REACH) | (own_row >= ROWS * tiles - REACH)
    second.wait_recv()
    halves = []
    for phase in range(2):
        theirs = jnp.concatenate([r2[0, phase], r2[1, phase]], axis=0)
        halves.append(both[phase] - 0.1 * jnp.where(edge_row, 0.0, theirs))
    result = pick(jnp.concatenate(halves, axis=1), table)

    mine[...] = result
    own = out.at[:, pl.ds(pl.multiple_of(CHUNK * c, CHUNK), CHUNK)]
    keep = pltpu.make_async_copy(mine, own, load_sem.at[4])
    gathers = {slot: go(remote(mine, own, gsend.at[slot], grecv.at[slot], peer(slot)[0])) for slot in order}
    keep.start()
    for copy in gathers.values():
        copy.wait_recv()
    keep.wait()
    for copy in started:
        copy.wait_send()


def local(tiles, estimate, frames, shifts, blur):
    vmem = lambda *shape: pltpu.VMEM(shape, F32)
    dma = lambda n: pltpu.SemaphoreType.DMA((n,))
    return pl.pallas_call(
        functools.partial(kernel, tiles),
        out_shape=jax.ShapeDtypeStruct(estimate.shape, F32),
        in_specs=[pl.BlockSpec(memory_space=pltpu.HBM)] * 4,
        out_specs=pl.BlockSpec(memory_space=pl.ANY),
        scratch_shapes=[
            pltpu.SMEM((TAPS,), F32),
            pltpu.SMEM((1, 2), jnp.int32),
            vmem(3 * ROWS, 768),
            vmem(8, FRAMES * LOW),
            vmem(8, FRAMES * LOW + 128),
            vmem(FRAMES, 2, 128),
            vmem(FRAMES, 8, LOW),
            vmem(FRAMES, 2, 128),
            vmem(128, 128),
            vmem(2, 3 * ROWS, 256),
            vmem(6, 3 * ROWS, 256),
            vmem(3, 3 * ROWS, 256),
            pltpu.VMEM((KDIM, 256), BF16),
            pltpu.VMEM((KDIM, 256), BF16),
            vmem(KDIM, 128),
            pltpu.VMEM((OFFS * BAND, 384), BF16),
            pltpu.VMEM((256, KDIM), BF16),
            vmem(OFFS * BAND, 256),
            vmem(2, BAND, 256),
            vmem(2, BAND, 256),
            vmem(2, 2, REACH, 128),
            vmem(2, 2, REACH, 128),
            vmem(2, BAND, 256),
            vmem(ROWS, CHUNK),
            dma(5), dma(2), dma(2), dma(FRAMES), dma(FRAMES), dma(FRAMES), dma(FRAMES),
            dma(2), dma(2), dma(2), dma(2), dma(FRAMES), dma(FRAMES),
        ],
        compiler_params=pltpu.CompilerParams(collective_id=0, has_side_effects=True, vmem_limit_bytes=16 * 1024 * 1024),
    )(*(pltpu.with_memory_space_constraint(value, pltpu.HBM) for value in (estimate, frames, shifts, blur)))


def solution(mesh):
    placed = (P("tile", None), P("frame", "tile", None), P("frame", None), P())
    return jax.shard_map(
        functools.partial(local, mesh.shape["tile"]),
        mesh=mesh, in_specs=placed, out_specs=P("tile", None), check_vma=False,
    )
```

```python
import functools

import jax
import jax.numpy as jnp
from jax import lax
from jax.experimental import pallas as pl
from jax.experimental.pallas import tpu as pltpu
from jax.sharding import PartitionSpec as P

RADIUS = 3
TAPS = 2 * RADIUS + 1
WINDOW = 2
REACH = 8
OFFS = 2 * REACH + 1
SIDE = 4
CHUNK = 256
LOW = CHUNK // 2
EDGE = 12
ROWS = 16
BAND = 2 * ROWS
SLOT = 32
FRAMES = SIDE * SIDE
KDIM = 640
MESH = pl.DeviceIdType.MESH
F32 = jnp.float32
BF16 = jnp.bfloat16


def iota(shape, axis):
    return lax.broadcasted_iota(jnp.int32, shape, axis)


def three(value):
    high = value.astype(BF16)
    rest = value - high.astype(F32)
    middle = rest.astype(BF16)
    low = (rest - middle.astype(F32)).astype(BF16)
    return jnp.concatenate([high, middle, low], axis=0)


def pick(value, table):
    rows = value.shape[0]
    out = jnp.dot(three(value), table, preferred_element_type=F32)
    return out[:rows] + out[rows : 2 * rows] + out[2 * rows :]


def left(value, amount):
    width = value.shape[1]
    return value if amount % width == 0 else pltpu.roll(value, (-amount) % width, 1)


def kernel(
    tiles, est, frames, shifts, blur, out,
    taps_in, shift_in, xw, fr, zs, zp, fb, hp, fh, xs, px, pg, xh, xl, aa, a3, af, hh, d1, r1, d2, r2, pr, mine,
    load_sem, hsend, hrecv, fsend, frecv, ssend, srecv,
    e1send, e1recv, e2send, e2recv, gsend, grecv,
):
    t = lax.axis_index("tile")
    f = lax.axis_index("frame")
    x = f // SIDE
    y = f % SIDE
    c = SIDE * y + x
    last = FRAMES - 1
    at_low = (last - c) // last
    at_high = c // last
    start = pl.multiple_of(128 * (2 * c - 1 + at_low - at_high), 128)
    lane0 = pl.multiple_of(128 * (1 + at_low - at_high), 128)
    up = lax.rem(t + tiles - 1, tiles)
    down = lax.rem(t + 1, tiles)

    def remote(src, dst, send, recv, device):
        return pltpu.make_async_remote_copy(
            src_ref=src, dst_ref=dst, send_sem=send, recv_sem=recv, device_id=device, device_id_type=MESH
        )

    def across_tiles(above, below):
        has_above, has_below = t > 0, t < tiles - 1

        class Pair:
            def start(self):
                pl.when(has_above)(above.start)
                pl.when(has_below)(below.start)

            def wait_recv(self):
                pl.when(has_above)(below.wait_recv)
                pl.when(has_below)(above.wait_recv)

            def wait_send(self):
                pl.when(has_above)(above.wait_send)
                pl.when(has_below)(below.wait_send)

        return Pair()

    def peer(slot):
        px_, py_ = lax.rem(x + slot // SIDE, SIDE), lax.rem(y + slot % SIDE, SIDE)
        return {"frame": SIDE * px_ + py_}, SIDE * py_ + px_

    order = sorted(range(1, FRAMES), key=lambda slot: -(min(slot // SIDE, 4 - slot // SIDE) + 2 * min(slot % SIDE, 4 - slot % SIDE)))

    window = est.at[:, pl.ds(start, 512)]
    load_f = pltpu.make_async_copy(frames.at[0], fr, load_sem.at[0])
    load_x = pltpu.make_async_copy(window, xw.at[pl.ds(ROWS, ROWS), pl.ds(lane0, 512)], load_sem.at[1])
    load_s = pltpu.make_async_copy(shifts, shift_in, load_sem.at[2])
    load_b = pltpu.make_async_copy(blur, taps_in, load_sem.at[3])

    barrier = pltpu.get_barrier_semaphore()

    def greet(device):
        pl.semaphore_signal(barrier, inc=1, device_id=device, device_id_type=MESH)

    load_f.start()
    load_s.start()
    for slot in order:
        greet(peer(slot)[0])
    pl.when(t > 0)(lambda: greet({"tile": up}))
    pl.when(t < tiles - 1)(lambda: greet({"tile": down}))
    load_x.start()
    load_b.start()

    load_f.wait()
    lane = iota((8, 128), 1)
    sub = iota((8, 128), 0)
    before = jnp.zeros((8, 128), F32)
    load_s.wait()
    tail = jnp.where(
        lane == 2 * EDGE, jnp.full((8, 128), shift_in[0, 0].astype(F32)), jnp.full((8, 128), shift_in[0, 1].astype(F32))
    )
    for tile in range(FRAMES + 1):
        rolled = pltpu.roll(fr[:, 128 * tile : 128 * tile + 128], EDGE, 1) if tile < FRAMES else jnp.zeros((8, 128), F32)
        zs[:, 128 * tile : 128 * tile + 128] = jnp.where(lane < EDGE, before, rolled)
        before = rolled
        if tile:
            part = jnp.where(lane < 2 * EDGE, zs[:, 128 * tile : 128 * tile + 128], tail)
            part = jnp.where(lane < SLOT, part, 0.0)
            for turn in range(1, 4):
                part = jnp.where(sub % 4 == turn, pltpu.roll(part, 128 - SLOT * turn, 1), part)
            zp[tile - 1, 0:1] = jnp.sum(jnp.where(sub < 4, part, 0.0), axis=0, keepdims=True)
            zp[tile - 1, 1:2] = jnp.sum(jnp.where(sub < 4, 0.0, part), axis=0, keepdims=True)
    pl.semaphore_wait(barrier, FRAMES + (t + tiles - 1) // tiles - (t + 1) // tiles)

    started = []

    def go(copy):
        copy.start()
        started.append(copy)
        return copy

    fcopies = {}
    scopies = {}
    for slot in order:
        device, chunk = peer(slot)
        scopies[slot] = go(remote(zp.at[chunk], hp.at[slot], ssend.at[slot], srecv.at[slot], device))
    for slot in order:
        device, chunk = peer(slot)
        source = zs.at[:, pl.ds(pl.multiple_of(LOW * chunk, LOW), LOW)]
        fcopies[slot] = go(remote(source, fb.at[slot], fsend.at[slot], frecv.at[slot], device))
    halo = go(
        across_tiles(
            remote(window, xw.at[pl.ds(2 * ROWS, ROWS), pl.ds(lane0, 512)], hsend.at[0], hrecv.at[1], {"tile": up}),
            remote(window, xw.at[pl.ds(0, ROWS), pl.ds(lane0, 512)], hsend.at[1], hrecv.at[0], {"tile": down}),
        )
    )
    fb[0] = zs[:, pl.ds(pl.multiple_of(LOW * c, LOW), LOW)]
    hp[0] = zp[c]

    high_cols = CHUNK * FRAMES
    load_x.wait()
    halo.wait_recv()
    row = ROWS * t - ROWS + iota((3 * ROWS, 512), 0)
    col = CHUNK * c - 128 + iota((3 * ROWS, 512), 1)
    inside = (row >= 0) & (row < ROWS * tiles) & (col >= 0) & (col < high_cols)
    raw = jnp.where(inside, xw[:, 128:640], 0.0)
    lane_in = iota((512, 256), 0)
    lane_out = iota((512, 256), 1)
    for phase in range(2):
        table = jnp.where(lane_in == 96 + phase + 2 * lane_out, 1.0, 0.0).astype(BF16)
        xs[phase] = pick(raw, table)

    row = ROWS * t - ROWS + iota((3 * ROWS, 256), 0)
    col = CHUNK * c - 32 + 2 * iota((3 * ROWS, 256), 1)
    inside = (row >= 0) & (row < ROWS * tiles) & (col >= 0) & (col < high_cols)
    gain = jnp.where(inside, 2.0, 1.0)
    pg[0] = left(gain, -1)
    pg[1] = gain
    pg[2] = left(gain, 1)

    def split(value):
        high = value.astype(BF16)
        return high, (value - high.astype(F32)).astype(BF16)

    def stage_model(lo):
        for off in range(OFFS):
            rows = slice(BAND * off, BAND * off + BAND)
            xh[rows], xl[rows] = split(left(xs[off % 2, lo : lo + BAND], off // 2))

    def stage_prior(lo, count):
        for phase in range(2):
            double = 2.0 * xs[phase, lo : lo + count]
            px[3 * phase, lo : lo + count] = left(double, -1)
            px[3 * phase + 1, lo : lo + count] = double
            px[3 * phase + 2, lo : lo + count] = left(double, 1)

    def prior(phase, lo, count):
        centre = px[3 * phase + 1, lo : lo + count]
        total = jnp.zeros((count, 256), F32)
        for side in range(-WINDOW, WINDOW + 1):
            other = (phase + side) % 2
            lanes = (phase + side - other) // 2 + 1
            for down_off in range(-WINDOW, WINDOW + 1):
                if down_off == 0 and side == 0:
                    continue
                rows = slice(lo + down_off, lo + down_off + count)
                weight = 0.7 ** (abs(down_off) + abs(side))
                slope = jnp.tanh(centre - px[3 * other + lanes, rows])
                total = total + (weight * slope) * pg[lanes, rows]
        return total

    xh[OFFS * BAND : KDIM] = jnp.zeros((KDIM - OFFS * BAND, 256), BF16)
    xl[OFFS * BAND : KDIM] = jnp.zeros((KDIM - OFFS * BAND, 256), BF16)
    aa[OFFS * BAND : KDIM] = jnp.zeros((KDIM - OFFS * BAND, 128), F32)
    stage_model(REACH)

    for copy in scopies.values():
        copy.wait_recv()
    frame = iota((1, 128), 1) // 8
    down_shift = jnp.zeros((1, 128), F32)
    side_shift = jnp.zeros((1, 128), F32)
    for slot in range(FRAMES):
        down_shift = jnp.where(frame == slot, hp[slot, 0:1, 2 * EDGE : 2 * EDGE + 1], down_shift)
        side_shift = jnp.where(frame == slot, hp[slot, 0:1, 2 * EDGE + 1 : 2 * EDGE + 2], side_shift)
        rows = jnp.where(
            sub < 4, jnp.broadcast_to(hp[slot, 0:1], (8, 128)), jnp.broadcast_to(hp[slot, 1:2], (8, 128))
        )
        for _ in range(2):
            rows = pltpu.roll(rows, 0, 1, stride=SLOT // 2, stride_axis=0)
        fh[8 * slot : 8 * slot + 8] = rows
    load_b.wait()
    blur_sum = taps_in[0]
    for tap in range(1, TAPS):
        blur_sum = blur_sum + taps_in[tap]
    scale = jnp.full((1, 128), blur_sum)
    taps = [jnp.full((1, 128), taps_in[tap]) / scale for tap in range(TAPS)]

    def tap_at(distance):
        total = jnp.zeros(distance.shape, F32)
        for tap in range(TAPS):
            total = jnp.where(distance == float(tap - RADIUS), jnp.broadcast_to(taps[tap], distance.shape), total)
        return total

    place = (iota((BAND, 128), 0) - REACH - 2 * (iota((BAND, 128), 1) % 8)).astype(F32)
    by_row = tap_at(place - down_shift)
    by_col = tap_at((iota((24, 128), 0) - REACH).astype(F32) - side_shift)
    for off in range(OFFS):
        rows = slice(BAND * off, BAND * off + BAND)
        entry = by_row * by_col[off : off + 1]
        aa[rows] = entry
        a3[rows, 0:128], a3[rows, 128:256] = split(entry)
        a3[rows, 256:384] = a3[rows, 0:128]
    for block in range(KDIM // 128):
        columns = slice(128 * block, 128 * block + 128)
        af[:128, columns], af[128:, columns] = split(aa[128 * block : 128 * block + 128].T)

    low = LOW * c - EDGE + iota((128, 256), 1)
    live = (low >= 0) & (low < LOW * FRAMES)

    def misfits():
        both = jnp.dot(af[...], xh[...], preferred_element_type=F32)
        return both[:128] + both[128:] + jnp.dot(af[:128], xl[...], preferred_element_type=F32)

    def adjoint(pred):
        seen = jnp.concatenate([fb[...].reshape(128, LOW), fh[...]], axis=1)
        high, rest = split(jnp.where(live, jnp.tanh(pred - seen), 0.0))
        hh[...] = jnp.dot(a3[...], jnp.concatenate([high, high, rest], axis=0), preferred_element_type=F32)

    pred = misfits()
    for copy in fcopies.values():
        copy.wait_recv()
    adjoint(pred)
    for phase in range(2):
        total = jnp.zeros((BAND, 256), F32)
        for off in range(phase, OFFS, 2):
            total = total + left(hh[BAND * off : BAND * off + BAND], -(off // 2))
        d1[phase] = total
    first = go(
        across_tiles(
            remote(d1.at[:, pl.ds(0, ROWS)], r1.at[:, pl.ds(ROWS, ROWS)], e1send.at[0], e1recv.at[1], {"tile": up}),
            remote(d1.at[:, pl.ds(ROWS, ROWS)], r1.at[:, pl.ds(0, ROWS)], e1send.at[1], e1recv.at[0], {"tile": down}),
        )
    )
    reach_row = ROWS * t - REACH + iota((BAND, 256), 0)
    edge_row = (reach_row < REACH) | (reach_row >= ROWS * tiles - REACH)
    within = pg[1, REACH : REACH + BAND] > 1.5
    stage_prior(0, 3 * ROWS)
    for phase in range(2):
        pr[phase] = xs[phase, REACH : REACH + BAND] - 0.005 * prior(phase, REACH, BAND)
    first.wait_recv()
    for phase in range(2):
        theirs = jnp.where(edge_row, 0.0, r1[phase])
        xs[phase, REACH : REACH + BAND] = jnp.where(within, pr[phase] - 0.1 * (d1[phase] + theirs), 0.0)

    stage_model(REACH)
    adjoint(misfits())
    both = []
    for phase in range(2):
        total = jnp.zeros((BAND, 128), F32)
        for off in range(phase, OFFS, 2):
            total = total + left(hh[BAND * off : BAND * off + BAND], ROWS - off // 2)[:, :128]
        d2[0, phase] = total[:REACH]
        d2[1, phase] = total[3 * REACH :]
        both.append(total[REACH : 3 * REACH])
    second = go(
        across_tiles(
            remote(d2.at[0], r2.at[1], e2send.at[0], e2recv.at[1], {"tile": up}),
            remote(d2.at[1], r2.at[0], e2send.at[1], e2recv.at[0], {"tile": down}),
        )
    )

    stage_prior(REACH, BAND)
    for phase in range(2):
        kept = xs[phase, ROWS : 2 * ROWS] - 0.005 * prior(phase, ROWS, ROWS)
        both[phase] = left(kept, ROWS)[:, :128] - 0.1 * both[phase]
    lane_in = iota((CHUNK, CHUNK), 0)
    lane_out = iota((CHUNK, CHUNK), 1)
    table = jnp.where(lane_out == jnp.where(lane_in < LOW, 2 * lane_in, 2 * lane_in - CHUNK + 1), 1.0, 0.0).astype(BF16)
    own_row = ROWS * t + iota((ROWS, LOW), 0)
    edge_row = (own_row < REACH) | (own_row >= ROWS * tiles - REACH)
    second.wait_recv()
    halves = []
    for phase in range(2):
        theirs = jnp.concatenate([r2[0, phase], r2[1, phase]], axis=0)
        halves.append(both[phase] - 0.1 * jnp.where(edge_row, 0.0, theirs))
    result = pick(jnp.concatenate(halves, axis=1), table)

    mine[...] = result
    own = out.at[:, pl.ds(pl.multiple_of(CHUNK * c, CHUNK), CHUNK)]
    keep = pltpu.make_async_copy(mine, own, load_sem.at[4])
    def gather(slot, source, target, device):
        return remote(source, target, gsend.at[slot], grecv.at[slot], device)

    direct = [gather(slot, mine, own, peer(slot)[0]) for slot in order]

    @pl.when(t % 4 != 1)
    def _():
        for copy in direct:
            copy.start()
        keep.start()
        for copy in direct:
            copy.wait_recv()
        for copy in direct:
            copy.wait_send()

    @pl.when(t % 4 == 1)
    def _():
        copies = {slot: copy for slot, copy in zip(order, direct) if slot < SIDE or slot % SIDE == 0}
        for slot in (2, 1, 3, 8, 4, 12):
            copies[slot].start()
        keep.start()
        for ey in (1, 3, 2):
            copies[ey].wait_recv()
            source = SIDE * lax.rem(y + SIDE - ey, SIDE) + x
            passing = out.at[:, pl.ds(pl.multiple_of(CHUNK * source, CHUNK), CHUNK)]
            for ex in (2, 1, 3):
                slot = SIDE * ex + ey
                copies[slot] = gather(slot, passing, passing, peer(SIDE * ex)[0])
                copies[slot].start()
        for slot, copy in copies.items():
            if slot >= SIDE:
                copy.wait_recv()
        for copy in copies.values():
            copy.wait_send()

    keep.wait()
    for copy in started:
        copy.wait_send()


def local(tiles, estimate, frames, shifts, blur):
    vmem = lambda *shape: pltpu.VMEM(shape, F32)
    dma = lambda n: pltpu.SemaphoreType.DMA((n,))
    return pl.pallas_call(
        functools.partial(kernel, tiles),
        out_shape=jax.ShapeDtypeStruct(estimate.shape, F32),
        in_specs=[pl.BlockSpec(memory_space=pltpu.HBM)] * 4,
        out_specs=pl.BlockSpec(memory_space=pl.ANY),
        scratch_shapes=[
            pltpu.SMEM((TAPS,), F32),
            pltpu.SMEM((1, 2), jnp.int32),
            vmem(3 * ROWS, 768),
            vmem(8, FRAMES * LOW),
            vmem(8, FRAMES * LOW + 128),
            vmem(FRAMES, 2, 128),
            vmem(FRAMES, 8, LOW),
            vmem(FRAMES, 2, 128),
            vmem(128, 128),
            vmem(2, 3 * ROWS, 256),
            vmem(6, 3 * ROWS, 256),
            vmem(3, 3 * ROWS, 256),
            pltpu.VMEM((KDIM, 256), BF16),
            pltpu.VMEM((KDIM, 256), BF16),
            vmem(KDIM, 128),
            pltpu.VMEM((OFFS * BAND, 384), BF16),
            pltpu.VMEM((256, KDIM), BF16),
            vmem(OFFS * BAND, 256),
            vmem(2, BAND, 256),
            vmem(2, BAND, 256),
            vmem(2, 2, REACH, 128),
            vmem(2, 2, REACH, 128),
            vmem(2, BAND, 256),
            vmem(ROWS, CHUNK),
            dma(5), dma(2), dma(2), dma(FRAMES), dma(FRAMES), dma(FRAMES), dma(FRAMES),
            dma(2), dma(2), dma(2), dma(2), dma(FRAMES), dma(FRAMES),
        ],
        compiler_params=pltpu.CompilerParams(collective_id=0, has_side_effects=True, vmem_limit_bytes=16 * 1024 * 1024),
    )(*(pltpu.with_memory_space_constraint(value, pltpu.HBM) for value in (estimate, frames, shifts, blur)))


def solution(mesh):
    placed = (P("tile", None), P("frame", "tile", None), P("frame", None), P())
    return jax.shard_map(
        functools.partial(local, mesh.shape["tile"]),
        mesh=mesh, in_specs=placed, out_specs=P("tile", None), check_vma=False,
    )
```

```python
import functools

import jax
import jax.numpy as jnp
from jax import lax
from jax.experimental import pallas as pl
from jax.experimental.pallas import tpu as pltpu
from jax.sharding import PartitionSpec as P

RADIUS = 3
TAPS = 2 * RADIUS + 1
WINDOW = 2
REACH = 8
OFFS = 2 * REACH + 1
SIDE = 4
CHUNK = 256
LOW = CHUNK // 2
EDGE = 12
ROWS = 16
BAND = 2 * ROWS
SLOT = 32
FRAMES = SIDE * SIDE
KDIM = 640
OUTER = OFFS * ROWS
MESH = pl.DeviceIdType.MESH
F32 = jnp.float32
BF16 = jnp.bfloat16


def iota(shape, axis):
    return lax.broadcasted_iota(jnp.int32, shape, axis)


def three(value):
    high = value.astype(BF16)
    rest = value - high.astype(F32)
    middle = rest.astype(BF16)
    low = (rest - middle.astype(F32)).astype(BF16)
    return jnp.concatenate([high, middle, low], axis=0)


def pick(value, table):
    rows = value.shape[0]
    out = jnp.dot(three(value), table, preferred_element_type=F32)
    return out[:rows] + out[rows : 2 * rows] + out[2 * rows :]


def left(value, amount):
    width = value.shape[1]
    return value if amount % width == 0 else pltpu.roll(value, (-amount) % width, 1)


def kernel(
    tiles, est, frames, shifts, blur, out,
    taps_in, shift_in, xw, fr, zs, zp, fb, hp, fh, xs, px, pg, xh, xl, aa, a3, af, hh, d1, r1, d2, r2, pr, mine,
    load_sem, hsend, hrecv, fsend, frecv, ssend, srecv,
    e1send, e1recv, e2send, e2recv, gsend, grecv,
):
    t = lax.axis_index("tile")
    f = lax.axis_index("frame")
    x = f // SIDE
    y = f % SIDE
    c = SIDE * y + x
    last = FRAMES - 1
    at_low = (last - c) // last
    at_high = c // last
    start = pl.multiple_of(128 * (2 * c - 1 + at_low - at_high), 128)
    lane0 = pl.multiple_of(128 * (1 + at_low - at_high), 128)
    up = lax.rem(t + tiles - 1, tiles)
    down = lax.rem(t + 1, tiles)

    def remote(src, dst, send, recv, device):
        return pltpu.make_async_remote_copy(
            src_ref=src, dst_ref=dst, send_sem=send, recv_sem=recv, device_id=device, device_id_type=MESH
        )

    def across_tiles(above, below):
        has_above, has_below = t > 0, t < tiles - 1

        class Pair:
            def start(self):
                pl.when(has_above)(above.start)
                pl.when(has_below)(below.start)

            def wait_recv(self):
                pl.when(has_above)(below.wait_recv)
                pl.when(has_below)(above.wait_recv)

            def wait_send(self):
                pl.when(has_above)(above.wait_send)
                pl.when(has_below)(below.wait_send)

        return Pair()

    def peer(slot):
        px_, py_ = lax.rem(x + slot // SIDE, SIDE), lax.rem(y + slot % SIDE, SIDE)
        return {"frame": SIDE * px_ + py_}, SIDE * py_ + px_

    order = sorted(range(1, FRAMES), key=lambda slot: -(min(slot // SIDE, 4 - slot // SIDE) + 2 * min(slot % SIDE, 4 - slot % SIDE)))

    window = est.at[:, pl.ds(start, 512)]
    load_f = pltpu.make_async_copy(frames.at[0], fr, load_sem.at[0])
    load_x = pltpu.make_async_copy(window, xw.at[pl.ds(ROWS, ROWS), pl.ds(lane0, 512)], load_sem.at[1])
    load_s = pltpu.make_async_copy(shifts, shift_in, load_sem.at[2])
    load_b = pltpu.make_async_copy(blur, taps_in, load_sem.at[3])

    barrier = pltpu.get_barrier_semaphore()

    def greet(device):
        pl.semaphore_signal(barrier, inc=1, device_id=device, device_id_type=MESH)

    load_f.start()
    load_s.start()
    for slot in order:
        greet(peer(slot)[0])
    pl.when(t > 0)(lambda: greet({"tile": up}))
    pl.when(t < tiles - 1)(lambda: greet({"tile": down}))
    load_x.start()
    load_b.start()

    load_f.wait()
    lane = iota((8, 128), 1)
    sub = iota((8, 128), 0)
    before = jnp.zeros((8, 128), F32)
    load_s.wait()
    tail = jnp.where(
        lane == 2 * EDGE, jnp.full((8, 128), shift_in[0, 0].astype(F32)), jnp.full((8, 128), shift_in[0, 1].astype(F32))
    )
    for tile in range(FRAMES + 1):
        rolled = pltpu.roll(fr[:, 128 * tile : 128 * tile + 128], EDGE, 1) if tile < FRAMES else jnp.zeros((8, 128), F32)
        zs[:, 128 * tile : 128 * tile + 128] = jnp.where(lane < EDGE, before, rolled)
        before = rolled
        if tile:
            part = jnp.where(lane < 2 * EDGE, zs[:, 128 * tile : 128 * tile + 128], tail)
            part = jnp.where(lane < SLOT, part, 0.0)
            for turn in range(1, 4):
                part = jnp.where(sub % 4 == turn, pltpu.roll(part, 128 - SLOT * turn, 1), part)
            zp[tile - 1, 0:1] = jnp.sum(jnp.where(sub < 4, part, 0.0), axis=0, keepdims=True)
            zp[tile - 1, 1:2] = jnp.sum(jnp.where(sub < 4, 0.0, part), axis=0, keepdims=True)
    pl.semaphore_wait(barrier, FRAMES + (t + tiles - 1) // tiles - (t + 1) // tiles)

    started = []

    def go(copy):
        copy.start()
        started.append(copy)
        return copy

    fcopies = {}
    scopies = {}
    for slot in order:
        device, chunk = peer(slot)
        scopies[slot] = go(remote(zp.at[chunk], hp.at[slot], ssend.at[slot], srecv.at[slot], device))
    for slot in order:
        device, chunk = peer(slot)
        source = zs.at[:, pl.ds(pl.multiple_of(LOW * chunk, LOW), LOW)]
        fcopies[slot] = go(remote(source, fb.at[slot], fsend.at[slot], frecv.at[slot], device))
    halo = go(
        across_tiles(
            remote(window, xw.at[pl.ds(2 * ROWS, ROWS), pl.ds(lane0, 512)], hsend.at[0], hrecv.at[1], {"tile": up}),
            remote(window, xw.at[pl.ds(0, ROWS), pl.ds(lane0, 512)], hsend.at[1], hrecv.at[0], {"tile": down}),
        )
    )
    fb[0] = zs[:, pl.ds(pl.multiple_of(LOW * c, LOW), LOW)]
    hp[0] = zp[c]

    high_cols = CHUNK * FRAMES
    load_x.wait()
    halo.wait_recv()
    row = ROWS * t - ROWS + iota((3 * ROWS, 512), 0)
    col = CHUNK * c - 128 + iota((3 * ROWS, 512), 1)
    inside = (row >= 0) & (row < ROWS * tiles) & (col >= 0) & (col < high_cols)
    raw = jnp.where(inside, xw[:, 128:640], 0.0)
    lane_in = iota((512, 256), 0)
    lane_out = iota((512, 256), 1)
    for phase in range(2):
        table = jnp.where(lane_in == 96 + phase + 2 * lane_out, 1.0, 0.0).astype(BF16)
        xs[phase] = pick(raw, table)

    row = ROWS * t - ROWS + iota((3 * ROWS, 256), 0)
    col = CHUNK * c - 32 + 2 * iota((3 * ROWS, 256), 1)
    inside = (row >= 0) & (row < ROWS * tiles) & (col >= 0) & (col < high_cols)
    gain = jnp.where(inside, 2.0, 1.0)
    pg[0] = left(gain, -1)
    pg[1] = gain
    pg[2] = left(gain, 1)

    def split(value):
        high = value.astype(BF16)
        return high, (value - high.astype(F32)).astype(BF16)

    def stage_model(lo):
        for off in range(OFFS):
            rows = slice(BAND * off, BAND * off + BAND)
            xh[rows], xl[rows] = split(left(xs[off % 2, lo : lo + BAND], off // 2))

    def stage_prior(lo, count):
        for phase in range(2):
            double = 2.0 * xs[phase, lo : lo + count]
            px[3 * phase, lo : lo + count] = left(double, -1)
            px[3 * phase + 1, lo : lo + count] = double
            px[3 * phase + 2, lo : lo + count] = left(double, 1)

    def prior(phase, lo, count):
        centre = px[3 * phase + 1, lo : lo + count]
        total = jnp.zeros((count, 256), F32)
        for side in range(-WINDOW, WINDOW + 1):
            other = (phase + side) % 2
            lanes = (phase + side - other) // 2 + 1
            for down_off in range(-WINDOW, WINDOW + 1):
                if down_off == 0 and side == 0:
                    continue
                rows = slice(lo + down_off, lo + down_off + count)
                weight = 0.7 ** (abs(down_off) + abs(side))
                slope = jnp.tanh(centre - px[3 * other + lanes, rows])
                total = total + (weight * slope) * pg[lanes, rows]
        return total

    xh[OFFS * BAND : KDIM] = jnp.zeros((KDIM - OFFS * BAND, 256), BF16)
    xl[OFFS * BAND : KDIM] = jnp.zeros((KDIM - OFFS * BAND, 256), BF16)
    aa[OFFS * BAND : KDIM] = jnp.zeros((KDIM - OFFS * BAND, 128), F32)
    stage_model(REACH)

    for copy in scopies.values():
        copy.wait_recv()
    frame = iota((1, 128), 1) // 8
    down_shift = jnp.zeros((1, 128), F32)
    side_shift = jnp.zeros((1, 128), F32)
    for slot in range(FRAMES):
        down_shift = jnp.where(frame == slot, hp[slot, 0:1, 2 * EDGE : 2 * EDGE + 1], down_shift)
        side_shift = jnp.where(frame == slot, hp[slot, 0:1, 2 * EDGE + 1 : 2 * EDGE + 2], side_shift)
        rows = jnp.where(
            sub < 4, jnp.broadcast_to(hp[slot, 0:1], (8, 128)), jnp.broadcast_to(hp[slot, 1:2], (8, 128))
        )
        for _ in range(2):
            rows = pltpu.roll(rows, 0, 1, stride=SLOT // 2, stride_axis=0)
        fh[8 * slot : 8 * slot + 8] = rows
    load_b.wait()
    blur_sum = taps_in[0]
    for tap in range(1, TAPS):
        blur_sum = blur_sum + taps_in[tap]
    scale = jnp.full((1, 128), blur_sum)
    taps = [jnp.full((1, 128), taps_in[tap]) / scale for tap in range(TAPS)]

    def tap_at(distance):
        total = jnp.zeros(distance.shape, F32)
        for tap in range(TAPS):
            total = jnp.where(distance == float(tap - RADIUS), jnp.broadcast_to(taps[tap], distance.shape), total)
        return total

    place = (iota((BAND, 128), 0) - REACH - 2 * (iota((BAND, 128), 1) % 8)).astype(F32)
    by_row = tap_at(place - down_shift)
    by_col = tap_at((iota((24, 128), 0) - REACH).astype(F32) - side_shift)
    for off in range(OFFS):
        rows = slice(BAND * off, BAND * off + BAND)
        entry = by_row * by_col[off : off + 1]
        aa[rows] = entry
        high, rest = split(entry)
        for begin, height, place_at in ((0, 8, ROWS * off), (8, ROWS, OUTER + ROWS * off), (24, 8, ROWS * off + 8)):
            into, of = slice(place_at, place_at + height), slice(begin, begin + height)
            a3[into, 0:128] = high[of]
            a3[into, 128:256] = rest[of]
            a3[into, 256:384] = high[of]
    for block in range(KDIM // 128):
        columns = slice(128 * block, 128 * block + 128)
        af[:128, columns], af[128:, columns] = split(aa[128 * block : 128 * block + 128].T)

    low = LOW * c - EDGE + iota((128, 256), 1)
    live = (low >= 0) & (low < LOW * FRAMES)

    def misfits():
        both = jnp.dot(af[...], xh[...], preferred_element_type=F32)
        return both[:128] + both[128:] + jnp.dot(af[:128], xl[...], preferred_element_type=F32)

    def adjoint(pred):
        seen = jnp.concatenate([fb[...].reshape(128, LOW), fh[...]], axis=1)
        high, rest = split(jnp.where(live, jnp.tanh(pred - seen), 0.0))
        return jnp.concatenate([high, high, rest], axis=0)

    def spread(block, gap, move, width):
        rows = slice(OUTER * block, OUTER * block + OUTER)
        hh[rows] = jnp.dot(a3[rows], gap, preferred_element_type=F32)
        sums = []
        for phase in range(2):
            total = jnp.zeros((ROWS, width), F32)
            for off in range(phase, OFFS, 2):
                at = OUTER * block + ROWS * off
                total = total + left(hh[at : at + ROWS], move - off // 2)[:, :width]
            sums.append(total)
        return sums

    pred = misfits()
    for copy in fcopies.values():
        copy.wait_recv()
    gap = adjoint(pred)
    outer, inner = spread(0, gap, 0, 256), spread(1, gap, 0, 256)
    for phase in range(2):
        d1[phase, :8] = outer[phase][:8]
        d1[phase, 8:24] = inner[phase]
        d1[phase, 24:] = outer[phase][8:]
    first = go(
        across_tiles(
            remote(d1.at[:, pl.ds(0, ROWS)], r1.at[:, pl.ds(ROWS, ROWS)], e1send.at[0], e1recv.at[1], {"tile": up}),
            remote(d1.at[:, pl.ds(ROWS, ROWS)], r1.at[:, pl.ds(0, ROWS)], e1send.at[1], e1recv.at[0], {"tile": down}),
        )
    )
    reach_row = ROWS * t - REACH + iota((BAND, 256), 0)
    edge_row = (reach_row < REACH) | (reach_row >= ROWS * tiles - REACH)
    within = pg[1, REACH : REACH + BAND] > 1.5
    stage_prior(0, 3 * ROWS)
    for phase in range(2):
        pr[phase] = xs[phase, REACH : REACH + BAND] - 0.005 * prior(phase, REACH, BAND)
    first.wait_recv()
    for phase in range(2):
        theirs = jnp.where(edge_row, 0.0, r1[phase])
        xs[phase, REACH : REACH + BAND] = jnp.where(within, pr[phase] - 0.1 * (d1[phase] + theirs), 0.0)

    stage_model(REACH)
    gap = adjoint(misfits())
    outer = spread(0, gap, ROWS, LOW)
    for phase in range(2):
        d2[0, phase] = outer[phase][:8]
        d2[1, phase] = outer[phase][8:]
    second = go(
        across_tiles(
            remote(d2.at[0], r2.at[1], e2send.at[0], e2recv.at[1], {"tile": up}),
            remote(d2.at[1], r2.at[0], e2send.at[1], e2recv.at[0], {"tile": down}),
        )
    )

    both = spread(1, gap, ROWS, LOW)
    stage_prior(REACH, BAND)
    for phase in range(2):
        kept = xs[phase, ROWS : 2 * ROWS] - 0.005 * prior(phase, ROWS, ROWS)
        both[phase] = left(kept, ROWS)[:, :128] - 0.1 * both[phase]
    lane_in = iota((CHUNK, CHUNK), 0)
    lane_out = iota((CHUNK, CHUNK), 1)
    table = jnp.where(lane_out == jnp.where(lane_in < LOW, 2 * lane_in, 2 * lane_in - CHUNK + 1), 1.0, 0.0).astype(BF16)
    own_row = ROWS * t + iota((ROWS, LOW), 0)
    edge_row = (own_row < REACH) | (own_row >= ROWS * tiles - REACH)
    second.wait_recv()
    halves = []
    for phase in range(2):
        theirs = jnp.concatenate([r2[0, phase], r2[1, phase]], axis=0)
        halves.append(both[phase] - 0.1 * jnp.where(edge_row, 0.0, theirs))
    result = pick(jnp.concatenate(halves, axis=1), table)

    mine[...] = result
    own = out.at[:, pl.ds(pl.multiple_of(CHUNK * c, CHUNK), CHUNK)]
    keep = pltpu.make_async_copy(mine, own, load_sem.at[4])
    def gather(slot, source, target, device):
        return remote(source, target, gsend.at[slot], grecv.at[slot], device)

    direct = [gather(slot, mine, own, peer(slot)[0]) for slot in order]

    @pl.when(t % 4 != 1)
    def _():
        for copy in direct:
            copy.start()
        keep.start()
        for copy in direct:
            copy.wait_recv()
        for copy in direct:
            copy.wait_send()

    @pl.when(t % 4 == 1)
    def _():
        copies = {slot: copy for slot, copy in zip(order, direct) if slot < SIDE or slot % SIDE == 0}
        for slot in (2, 1, 3, 8, 4, 12):
            copies[slot].start()
        keep.start()
        for ey in (1, 3, 2):
            copies[ey].wait_recv()
            source = SIDE * lax.rem(y + SIDE - ey, SIDE) + x
            passing = out.at[:, pl.ds(pl.multiple_of(CHUNK * source, CHUNK), CHUNK)]
            for ex in (2, 1, 3):
                slot = SIDE * ex + ey
                copies[slot] = gather(slot, passing, passing, peer(SIDE * ex)[0])
                copies[slot].start()
        for slot, copy in copies.items():
            if slot >= SIDE:
                copy.wait_recv()
        for copy in copies.values():
            copy.wait_send()

    keep.wait()
    for copy in started:
        copy.wait_send()


def local(tiles, estimate, frames, shifts, blur):
    vmem = lambda *shape: pltpu.VMEM(shape, F32)
    dma = lambda n: pltpu.SemaphoreType.DMA((n,))
    return pl.pallas_call(
        functools.partial(kernel, tiles),
        out_shape=jax.ShapeDtypeStruct(estimate.shape, F32),
        in_specs=[pl.BlockSpec(memory_space=pltpu.HBM)] * 4,
        out_specs=pl.BlockSpec(memory_space=pl.ANY),
        scratch_shapes=[
            pltpu.SMEM((TAPS,), F32),
            pltpu.SMEM((1, 2), jnp.int32),
            vmem(3 * ROWS, 768),
            vmem(8, FRAMES * LOW),
            vmem(8, FRAMES * LOW + 128),
            vmem(FRAMES, 2, 128),
            vmem(FRAMES, 8, LOW),
            vmem(FRAMES, 2, 128),
            vmem(128, 128),
            vmem(2, 3 * ROWS, 256),
            vmem(6, 3 * ROWS, 256),
            vmem(3, 3 * ROWS, 256),
            pltpu.VMEM((KDIM, 256), BF16),
            pltpu.VMEM((KDIM, 256), BF16),
            vmem(KDIM, 128),
            pltpu.VMEM((OFFS * BAND, 384), BF16),
            pltpu.VMEM((256, KDIM), BF16),
            vmem(OFFS * BAND, 256),
            vmem(2, BAND, 256),
            vmem(2, BAND, 256),
            vmem(2, 2, REACH, 128),
            vmem(2, 2, REACH, 128),
            vmem(2, BAND, 256),
            vmem(ROWS, CHUNK),
            dma(5), dma(2), dma(2), dma(FRAMES), dma(FRAMES), dma(FRAMES), dma(FRAMES),
            dma(2), dma(2), dma(2), dma(2), dma(FRAMES), dma(FRAMES),
        ],
        compiler_params=pltpu.CompilerParams(collective_id=0, has_side_effects=True, vmem_limit_bytes=16 * 1024 * 1024),
    )(*(pltpu.with_memory_space_constraint(value, pltpu.HBM) for value in (estimate, frames, shifts, blur)))


def solution(mesh):
    placed = (P("tile", None), P("frame", "tile", None), P("frame", None), P())
    return jax.shard_map(
        functools.partial(local, mesh.shape["tile"]),
        mesh=mesh, in_specs=placed, out_specs=P("tile", None), check_vma=False,
    )
```

```python
import functools

import jax
import jax.numpy as jnp
from jax import lax
from jax.experimental import pallas as pl
from jax.experimental.pallas import tpu as pltpu
from jax.sharding import PartitionSpec as P

RADIUS = 3
TAPS = 2 * RADIUS + 1
WINDOW = 2
REACH = 8
OFFS = 2 * REACH + 1
SIDE = 4
CHUNK = 256
LOW = CHUNK // 2
EDGE = 12
ROWS = 16
BAND = 2 * ROWS
SLOT = 32
FRAMES = SIDE * SIDE
KDIM = 640
OUTER = OFFS * ROWS
MESH = pl.DeviceIdType.MESH
F32 = jnp.float32
BF16 = jnp.bfloat16


def iota(shape, axis):
    return lax.broadcasted_iota(jnp.int32, shape, axis)


def three(value):
    high = value.astype(BF16)
    rest = value - high.astype(F32)
    middle = rest.astype(BF16)
    low = (rest - middle.astype(F32)).astype(BF16)
    return jnp.concatenate([high, middle, low], axis=0)


def pick(value, table):
    rows = value.shape[0]
    out = jnp.dot(three(value), table, preferred_element_type=F32)
    return out[:rows] + out[rows : 2 * rows] + out[2 * rows :]


def left(value, amount):
    width = value.shape[1]
    return value if amount % width == 0 else pltpu.roll(value, (-amount) % width, 1)


def kernel(
    tiles, est, frames, shifts, blur, out,
    taps_in, shift_in, xw, fr, zs, zp, fb, hp, fh, xs, px, pg, xh, xl, aa, a3, af, hh, d1, r1, d2, r2, pr, mine,
    load_sem, hsend, hrecv, fsend, frecv, ssend, srecv,
    e1send, e1recv, e2send, e2recv, gsend, grecv,
):
    t = lax.axis_index("tile")
    f = lax.axis_index("frame")
    x = f // SIDE
    y = f % SIDE
    c = SIDE * y + x
    last = FRAMES - 1
    at_low = (last - c) // last
    at_high = c // last
    start = pl.multiple_of(128 * (2 * c - 1 + at_low - at_high), 128)
    lane0 = pl.multiple_of(128 * (1 + at_low - at_high), 128)
    up = lax.rem(t + tiles - 1, tiles)
    down = lax.rem(t + 1, tiles)

    def remote(src, dst, send, recv, device):
        return pltpu.make_async_remote_copy(
            src_ref=src, dst_ref=dst, send_sem=send, recv_sem=recv, device_id=device, device_id_type=MESH
        )

    def across_tiles(above, below):
        has_above, has_below = t > 0, t < tiles - 1

        class Pair:
            def start(self):
                pl.when(has_above)(above.start)
                pl.when(has_below)(below.start)

            def wait_recv(self):
                pl.when(has_above)(below.wait_recv)
                pl.when(has_below)(above.wait_recv)

            def wait_send(self):
                pl.when(has_above)(above.wait_send)
                pl.when(has_below)(below.wait_send)

        return Pair()

    def peer(slot):
        px_, py_ = lax.rem(x + slot // SIDE, SIDE), lax.rem(y + slot % SIDE, SIDE)
        return {"frame": SIDE * px_ + py_}, SIDE * py_ + px_

    order = sorted(range(1, FRAMES), key=lambda slot: -(min(slot // SIDE, 4 - slot // SIDE) + 2 * min(slot % SIDE, 4 - slot % SIDE)))

    window = est.at[:, pl.ds(start, 512)]
    load_f = pltpu.make_async_copy(frames.at[0], fr, load_sem.at[0])
    load_x = pltpu.make_async_copy(window, xw.at[pl.ds(ROWS, ROWS), pl.ds(lane0, 512)], load_sem.at[1])
    load_s = pltpu.make_async_copy(shifts, shift_in, load_sem.at[2])
    load_b = pltpu.make_async_copy(blur, taps_in, load_sem.at[3])

    barrier = pltpu.get_barrier_semaphore()

    def greet(device):
        pl.semaphore_signal(barrier, inc=1, device_id=device, device_id_type=MESH)

    load_f.start()
    load_s.start()
    for slot in order:
        greet(peer(slot)[0])
    pl.when(t > 0)(lambda: greet({"tile": up}))
    pl.when(t < tiles - 1)(lambda: greet({"tile": down}))
    load_x.start()
    load_b.start()

    load_f.wait()
    lane = iota((8, 128), 1)
    sub = iota((8, 128), 0)
    before = jnp.zeros((8, 128), F32)
    load_s.wait()
    tail = jnp.where(
        lane == 2 * EDGE, jnp.full((8, 128), shift_in[0, 0].astype(F32)), jnp.full((8, 128), shift_in[0, 1].astype(F32))
    )
    for tile in range(FRAMES + 1):
        rolled = pltpu.roll(fr[:, 128 * tile : 128 * tile + 128], EDGE, 1) if tile < FRAMES else jnp.zeros((8, 128), F32)
        zs[:, 128 * tile : 128 * tile + 128] = jnp.where(lane < EDGE, before, rolled)
        before = rolled
        if tile:
            part = jnp.where(lane < 2 * EDGE, zs[:, 128 * tile : 128 * tile + 128], tail)
            part = jnp.where(lane < SLOT, part, 0.0)
            for turn in range(1, 4):
                part = jnp.where(sub % 4 == turn, pltpu.roll(part, 128 - SLOT * turn, 1), part)
            zp[tile - 1, 0:1] = jnp.sum(jnp.where(sub < 4, part, 0.0), axis=0, keepdims=True)
            zp[tile - 1, 1:2] = jnp.sum(jnp.where(sub < 4, 0.0, part), axis=0, keepdims=True)
    pl.semaphore_wait(barrier, FRAMES + (t + tiles - 1) // tiles - (t + 1) // tiles)

    started = []

    def go(copy):
        copy.start()
        started.append(copy)
        return copy

    fcopies = {}
    scopies = {}
    for slot in order:
        device, chunk = peer(slot)
        scopies[slot] = go(remote(zp.at[chunk], hp.at[slot], ssend.at[slot], srecv.at[slot], device))
    for slot in order:
        device, chunk = peer(slot)
        source = zs.at[:, pl.ds(pl.multiple_of(LOW * chunk, LOW), LOW)]
        fcopies[slot] = go(remote(source, fb.at[slot], fsend.at[slot], frecv.at[slot], device))
    halo = go(
        across_tiles(
            remote(window, xw.at[pl.ds(2 * ROWS, ROWS), pl.ds(lane0, 512)], hsend.at[0], hrecv.at[1], {"tile": up}),
            remote(window, xw.at[pl.ds(0, ROWS), pl.ds(lane0, 512)], hsend.at[1], hrecv.at[0], {"tile": down}),
        )
    )
    fb[0] = zs[:, pl.ds(pl.multiple_of(LOW * c, LOW), LOW)]
    hp[0] = zp[c]

    high_cols = CHUNK * FRAMES
    load_x.wait()
    halo.wait_recv()
    row = ROWS * t - ROWS + iota((3 * ROWS, 512), 0)
    col = CHUNK * c - 128 + iota((3 * ROWS, 512), 1)
    inside = (row >= 0) & (row < ROWS * tiles) & (col >= 0) & (col < high_cols)
    raw = jnp.where(inside, xw[:, 128:640], 0.0)
    lane_in = iota((512, 256), 0)
    lane_out = iota((512, 256), 1)
    for phase in range(2):
        table = jnp.where(lane_in == 96 + phase + 2 * lane_out, 1.0, 0.0).astype(BF16)
        xs[phase] = pick(raw, table)

    row = ROWS * t - ROWS + iota((3 * ROWS, 256), 0)
    col = CHUNK * c - 32 + 2 * iota((3 * ROWS, 256), 1)
    inside = (row >= 0) & (row < ROWS * tiles) & (col >= 0) & (col < high_cols)
    gain = jnp.where(inside, 2.0, 1.0)
    pg[0] = left(gain, -1)
    pg[1] = gain
    pg[2] = left(gain, 1)

    def split(value):
        high = value.astype(BF16)
        return high, (value - high.astype(F32)).astype(BF16)

    def stage_model(lo):
        for off in range(OFFS):
            rows = slice(BAND * off, BAND * off + BAND)
            xh[rows], xl[rows] = split(left(xs[off % 2, lo : lo + BAND], off // 2))

    def stage_prior(lo, count):
        for phase in range(2):
            double = 2.0 * xs[phase, lo : lo + count]
            px[3 * phase, lo : lo + count] = left(double, -1)
            px[3 * phase + 1, lo : lo + count] = double
            px[3 * phase + 2, lo : lo + count] = left(double, 1)

    def prior(phase, lo, count):
        centre = px[3 * phase + 1, lo : lo + count]
        total = jnp.zeros((count, 256), F32)
        for side in range(-WINDOW, WINDOW + 1):
            other = (phase + side) % 2
            lanes = (phase + side - other) // 2 + 1
            for down_off in range(-WINDOW, WINDOW + 1):
                if down_off == 0 and side == 0:
                    continue
                rows = slice(lo + down_off, lo + down_off + count)
                weight = 0.7 ** (abs(down_off) + abs(side))
                slope = jnp.tanh(centre - px[3 * other + lanes, rows])
                total = total + (weight * slope) * pg[lanes, rows]
        return total

    xh[OFFS * BAND : KDIM] = jnp.zeros((KDIM - OFFS * BAND, 256), BF16)
    xl[OFFS * BAND : KDIM] = jnp.zeros((KDIM - OFFS * BAND, 256), BF16)
    aa[OFFS * BAND : KDIM] = jnp.zeros((KDIM - OFFS * BAND, 128), F32)
    stage_model(REACH)

    for copy in scopies.values():
        copy.wait_recv()
    frame = iota((1, 128), 1) // 8
    down_shift = jnp.zeros((1, 128), F32)
    side_shift = jnp.zeros((1, 128), F32)
    for slot in range(FRAMES):
        down_shift = jnp.where(frame == slot, hp[slot, 0:1, 2 * EDGE : 2 * EDGE + 1], down_shift)
        side_shift = jnp.where(frame == slot, hp[slot, 0:1, 2 * EDGE + 1 : 2 * EDGE + 2], side_shift)
        rows = jnp.where(
            sub < 4, jnp.broadcast_to(hp[slot, 0:1], (8, 128)), jnp.broadcast_to(hp[slot, 1:2], (8, 128))
        )
        for _ in range(2):
            rows = pltpu.roll(rows, 0, 1, stride=SLOT // 2, stride_axis=0)
        fh[8 * slot : 8 * slot + 8] = rows
    load_b.wait()
    blur_sum = taps_in[0]
    for tap in range(1, TAPS):
        blur_sum = blur_sum + taps_in[tap]
    scale = jnp.full((1, 128), blur_sum)
    taps = [jnp.full((1, 128), taps_in[tap]) / scale for tap in range(TAPS)]

    def tap_at(distance):
        total = jnp.zeros(distance.shape, F32)
        for tap in range(TAPS):
            total = jnp.where(distance == float(tap - RADIUS), jnp.broadcast_to(taps[tap], distance.shape), total)
        return total

    place = (iota((BAND, 128), 0) - REACH - 2 * (iota((BAND, 128), 1) % 8)).astype(F32)
    by_row = tap_at(place - down_shift)
    by_col = tap_at((iota((24, 128), 0) - REACH).astype(F32) - side_shift)
    for off in range(OFFS):
        rows = slice(BAND * off, BAND * off + BAND)
        entry = by_row * by_col[off : off + 1]
        aa[rows] = entry
        high, rest = split(entry)
        for begin, height, place_at in ((0, 8, ROWS * off), (8, ROWS, OUTER + ROWS * off), (24, 8, ROWS * off + 8)):
            into, of = slice(place_at, place_at + height), slice(begin, begin + height)
            a3[into, 0:128] = high[of]
            a3[into, 128:256] = rest[of]
            a3[into, 256:384] = high[of]
    for block in range(KDIM // 128):
        columns = slice(128 * block, 128 * block + 128)
        af[:128, columns], af[128:, columns] = split(aa[128 * block : 128 * block + 128].T)

    low = LOW * c - EDGE + iota((128, 256), 1)
    live = (low >= 0) & (low < LOW * FRAMES)

    def misfits():
        both = jnp.dot(af[...], xh[...], preferred_element_type=F32)
        return both[:128] + both[128:] + jnp.dot(af[:128], xl[...], preferred_element_type=F32)

    def adjoint(pred):
        seen = jnp.concatenate([fb[...].reshape(128, LOW), fh[...]], axis=1)
        high, rest = split(jnp.where(live, jnp.tanh(pred - seen), 0.0))
        return jnp.concatenate([high, high, rest], axis=0)

    def spread(block, gap, move, width):
        rows = slice(OUTER * block, OUTER * block + OUTER)
        hh[rows] = jnp.dot(a3[rows], gap, preferred_element_type=F32)
        sums = []
        for phase in range(2):
            total = jnp.zeros((ROWS, width), F32)
            for off in range(phase, OFFS, 2):
                at = OUTER * block + ROWS * off
                total = total + left(hh[at : at + ROWS], move - off // 2)[:, :width]
            sums.append(total)
        return sums

    pred = misfits()
    for copy in fcopies.values():
        copy.wait_recv()
    gap = adjoint(pred)
    outer, inner = spread(0, gap, 0, 256), spread(1, gap, 0, 256)
    for phase in range(2):
        d1[phase, :8] = outer[phase][:8]
        d1[phase, 8:24] = inner[phase]
        d1[phase, 24:] = outer[phase][8:]
    first = go(
        across_tiles(
            remote(d1.at[:, pl.ds(0, ROWS)], r1.at[:, pl.ds(ROWS, ROWS)], e1send.at[0], e1recv.at[1], {"tile": up}),
            remote(d1.at[:, pl.ds(ROWS, ROWS)], r1.at[:, pl.ds(0, ROWS)], e1send.at[1], e1recv.at[0], {"tile": down}),
        )
    )
    reach_row = ROWS * t - REACH + iota((BAND, 256), 0)
    edge_row = (reach_row < REACH) | (reach_row >= ROWS * tiles - REACH)
    within = pg[1, REACH : REACH + BAND] > 1.5
    stage_prior(0, 3 * ROWS)
    for phase in range(2):
        pr[phase] = xs[phase, REACH : REACH + BAND] - 0.005 * prior(phase, REACH, BAND)
    first.wait_recv()
    for phase in range(2):
        theirs = jnp.where(edge_row, 0.0, r1[phase])
        xs[phase, REACH : REACH + BAND] = jnp.where(within, pr[phase] - 0.1 * (d1[phase] + theirs), 0.0)

    stage_model(REACH)
    gap = adjoint(misfits())
    outer = spread(0, gap, ROWS, LOW)
    for phase in range(2):
        d2[0, phase] = outer[phase][:8]
        d2[1, phase] = outer[phase][8:]
    second = go(
        across_tiles(
            remote(d2.at[0], r2.at[1], e2send.at[0], e2recv.at[1], {"tile": up}),
            remote(d2.at[1], r2.at[0], e2send.at[1], e2recv.at[0], {"tile": down}),
        )
    )

    both = spread(1, gap, ROWS, LOW)
    stage_prior(REACH, BAND)
    for phase in range(2):
        kept = xs[phase, ROWS : 2 * ROWS] - 0.005 * prior(phase, ROWS, ROWS)
        both[phase] = left(kept, ROWS)[:, :128] - 0.1 * both[phase]
    lane_in = iota((CHUNK, CHUNK), 0)
    lane_out = iota((CHUNK, CHUNK), 1)
    table = jnp.where(lane_out == jnp.where(lane_in < LOW, 2 * lane_in, 2 * lane_in - CHUNK + 1), 1.0, 0.0).astype(BF16)
    own_row = ROWS * t + iota((ROWS, LOW), 0)
    edge_row = (own_row < REACH) | (own_row >= ROWS * tiles - REACH)
    second.wait_recv()
    halves = []
    for phase in range(2):
        theirs = jnp.concatenate([r2[0, phase], r2[1, phase]], axis=0)
        halves.append(both[phase] - 0.1 * jnp.where(edge_row, 0.0, theirs))
    result = pick(jnp.concatenate(halves, axis=1), table)

    mine[...] = result
    own = out.at[:, pl.ds(pl.multiple_of(CHUNK * c, CHUNK), CHUNK)]
    keep = pltpu.make_async_copy(mine, own, load_sem.at[4])
    def gather(slot, source, target, device):
        return remote(source, target, gsend.at[slot], grecv.at[slot], device)

    direct = [gather(slot, mine, own, peer(slot)[0]) for slot in order]

    relays = (t % 2 == 1) & (t != tiles // 2 - 1)
    @pl.when(jnp.logical_not(relays))
    def _():
        for copy in direct:
            copy.start()
        keep.start()
        for copy in direct:
            copy.wait_recv()
        for copy in direct:
            copy.wait_send()

    @pl.when(relays)
    def _():
        copies = {slot: copy for slot, copy in zip(order, direct) if slot < SIDE or slot % SIDE == 0}
        for slot in (2, 1, 3, 8, 4, 12):
            copies[slot].start()
        keep.start()
        for ey in (1, 3, 2):
            copies[ey].wait_recv()
            source = SIDE * lax.rem(y + SIDE - ey, SIDE) + x
            passing = out.at[:, pl.ds(pl.multiple_of(CHUNK * source, CHUNK), CHUNK)]
            for ex in (2, 1, 3):
                slot = SIDE * ex + ey
                copies[slot] = gather(slot, passing, passing, peer(SIDE * ex)[0])
                copies[slot].start()
        for slot, copy in copies.items():
            if slot >= SIDE:
                copy.wait_recv()
        for copy in copies.values():
            copy.wait_send()

    keep.wait()
    for copy in started:
        copy.wait_send()


def local(tiles, estimate, frames, shifts, blur):
    vmem = lambda *shape: pltpu.VMEM(shape, F32)
    dma = lambda n: pltpu.SemaphoreType.DMA((n,))
    return pl.pallas_call(
        functools.partial(kernel, tiles),
        out_shape=jax.ShapeDtypeStruct(estimate.shape, F32),
        in_specs=[pl.BlockSpec(memory_space=pltpu.HBM)] * 4,
        out_specs=pl.BlockSpec(memory_space=pl.ANY),
        scratch_shapes=[
            pltpu.SMEM((TAPS,), F32),
            pltpu.SMEM((1, 2), jnp.int32),
            vmem(3 * ROWS, 768),
            vmem(8, FRAMES * LOW),
            vmem(8, FRAMES * LOW + 128),
            vmem(FRAMES, 2, 128),
            vmem(FRAMES, 8, LOW),
            vmem(FRAMES, 2, 128),
            vmem(128, 128),
            vmem(2, 3 * ROWS, 256),
            vmem(6, 3 * ROWS, 256),
            vmem(3, 3 * ROWS, 256),
            pltpu.VMEM((KDIM, 256), BF16),
            pltpu.VMEM((KDIM, 256), BF16),
            vmem(KDIM, 128),
            pltpu.VMEM((OFFS * BAND, 384), BF16),
            pltpu.VMEM((256, KDIM), BF16),
            vmem(OFFS * BAND, 256),
            vmem(2, BAND, 256),
            vmem(2, BAND, 256),
            vmem(2, 2, REACH, 128),
            vmem(2, 2, REACH, 128),
            vmem(2, BAND, 256),
            vmem(ROWS, CHUNK),
            dma(5), dma(2), dma(2), dma(FRAMES), dma(FRAMES), dma(FRAMES), dma(FRAMES),
            dma(2), dma(2), dma(2), dma(2), dma(FRAMES), dma(FRAMES),
        ],
        compiler_params=pltpu.CompilerParams(collective_id=0, has_side_effects=True, vmem_limit_bytes=16 * 1024 * 1024),
    )(*(pltpu.with_memory_space_constraint(value, pltpu.HBM) for value in (estimate, frames, shifts, blur)))


def solution(mesh):
    placed = (P("tile", None), P("frame", "tile", None), P("frame", None), P())
    return jax.shard_map(
        functools.partial(local, mesh.shape["tile"]),
        mesh=mesh, in_specs=placed, out_specs=P("tile", None), check_vma=False,
    )
```

```python
import functools

import jax
import jax.numpy as jnp
from jax import lax
from jax.experimental import pallas as pl
from jax.experimental.pallas import tpu as pltpu
from jax.sharding import PartitionSpec as P

RADIUS = 3
TAPS = 2 * RADIUS + 1
WINDOW = 2
REACH = 8
OFFS = 2 * REACH + 1
SIDE = 4
CHUNK = 256
LOW = CHUNK // 2
EDGE = 12
ROWS = 16
BAND = 2 * ROWS
SLOT = 32
FRAMES = SIDE * SIDE
KDIM = 640
GROUP = 8 * (OFFS + 1)
GROUPS = (1, 0, 3, 2)
MESH = pl.DeviceIdType.MESH
F32 = jnp.float32
BF16 = jnp.bfloat16


def iota(shape, axis):
    return lax.broadcasted_iota(jnp.int32, shape, axis)


def three(value):
    high = value.astype(BF16)
    rest = value - high.astype(F32)
    middle = rest.astype(BF16)
    low = (rest - middle.astype(F32)).astype(BF16)
    return jnp.concatenate([high, middle, low], axis=0)


def pick(value, table):
    rows = value.shape[0]
    out = jnp.dot(three(value), table, preferred_element_type=F32)
    return out[:rows] + out[rows : 2 * rows] + out[2 * rows :]


def left(value, amount):
    width = value.shape[1]
    return value if amount % width == 0 else pltpu.roll(value, (-amount) % width, 1)


def kernel(
    tiles, est, frames, shifts, blur, out,
    taps_in, shift_in, xw, fr, zs, zp, fb, hp, fh, xs, px, pg, xh, xl, aa, a3, af, hh, d1, r1, d2, r2, pr, mine,
    load_sem, hsend, hrecv, fsend, frecv, ssend, srecv,
    e1send, e1recv, e2send, e2recv, gsend, grecv,
):
    t = lax.axis_index("tile")
    f = lax.axis_index("frame")
    x = f // SIDE
    y = f % SIDE
    c = SIDE * y + x
    last = FRAMES - 1
    at_low = (last - c) // last
    at_high = c // last
    start = pl.multiple_of(128 * (2 * c - 1 + at_low - at_high), 128)
    lane0 = pl.multiple_of(128 * (1 + at_low - at_high), 128)
    up = lax.rem(t + tiles - 1, tiles)
    down = lax.rem(t + 1, tiles)

    def remote(src, dst, send, recv, device):
        return pltpu.make_async_remote_copy(
            src_ref=src, dst_ref=dst, send_sem=send, recv_sem=recv, device_id=device, device_id_type=MESH
        )

    def across_tiles(above, below):
        has_above, has_below = t > 0, t < tiles - 1

        class Pair:
            def start(self):
                pl.when(has_above)(above.start)
                pl.when(has_below)(below.start)

            def wait_recv(self):
                pl.when(has_above)(below.wait_recv)
                pl.when(has_below)(above.wait_recv)

            def wait_send(self):
                pl.when(has_above)(above.wait_send)
                pl.when(has_below)(below.wait_send)

        pair = Pair()
        pair.above, pair.below = above, below
        return pair

    def peer(slot):
        px_, py_ = lax.rem(x + slot // SIDE, SIDE), lax.rem(y + slot % SIDE, SIDE)
        return {"frame": SIDE * px_ + py_}, SIDE * py_ + px_

    order = sorted(range(1, FRAMES), key=lambda slot: -(min(slot // SIDE, 4 - slot // SIDE) + 2 * min(slot % SIDE, 4 - slot % SIDE)))

    window = est.at[:, pl.ds(start, 512)]
    load_f = pltpu.make_async_copy(frames.at[0], fr, load_sem.at[0])
    load_x = pltpu.make_async_copy(window, xw.at[pl.ds(ROWS, ROWS), pl.ds(lane0, 512)], load_sem.at[1])
    load_s = pltpu.make_async_copy(shifts, shift_in, load_sem.at[2])
    load_b = pltpu.make_async_copy(blur, taps_in, load_sem.at[3])

    barrier = pltpu.get_barrier_semaphore()

    def greet(device):
        pl.semaphore_signal(barrier, inc=1, device_id=device, device_id_type=MESH)

    load_f.start()
    load_s.start()
    for slot in order:
        greet(peer(slot)[0])
    pl.when(t > 0)(lambda: greet({"tile": up}))
    pl.when(t < tiles - 1)(lambda: greet({"tile": down}))
    load_x.start()
    load_b.start()

    load_f.wait()
    lane = iota((8, 128), 1)
    sub = iota((8, 128), 0)
    before = jnp.zeros((8, 128), F32)
    load_s.wait()
    tail = jnp.where(
        lane == 2 * EDGE, jnp.full((8, 128), shift_in[0, 0].astype(F32)), jnp.full((8, 128), shift_in[0, 1].astype(F32))
    )
    for tile in range(FRAMES + 1):
        rolled = pltpu.roll(fr[:, 128 * tile : 128 * tile + 128], EDGE, 1) if tile < FRAMES else jnp.zeros((8, 128), F32)
        zs[:, 128 * tile : 128 * tile + 128] = jnp.where(lane < EDGE, before, rolled)
        before = rolled
        if tile:
            part = jnp.where(lane < 2 * EDGE, zs[:, 128 * tile : 128 * tile + 128], tail)
            part = jnp.where(lane < SLOT, part, 0.0)
            for turn in range(1, 4):
                part = jnp.where(sub % 4 == turn, pltpu.roll(part, 128 - SLOT * turn, 1), part)
            zp[tile - 1, 0:1] = jnp.sum(jnp.where(sub < 4, part, 0.0), axis=0, keepdims=True)
            zp[tile - 1, 1:2] = jnp.sum(jnp.where(sub < 4, 0.0, part), axis=0, keepdims=True)
    pl.semaphore_wait(barrier, FRAMES + (t + tiles - 1) // tiles - (t + 1) // tiles)

    started = []

    def go(copy):
        copy.start()
        started.append(copy)
        return copy

    fcopies = {}
    scopies = {}
    for slot in order:
        device, chunk = peer(slot)
        scopies[slot] = go(remote(zp.at[chunk], hp.at[slot], ssend.at[slot], srecv.at[slot], device))
    for slot in order:
        device, chunk = peer(slot)
        source = zs.at[:, pl.ds(pl.multiple_of(LOW * chunk, LOW), LOW)]
        fcopies[slot] = go(remote(source, fb.at[slot], fsend.at[slot], frecv.at[slot], device))
    halo = go(
        across_tiles(
            remote(window, xw.at[pl.ds(2 * ROWS, ROWS), pl.ds(lane0, 512)], hsend.at[0], hrecv.at[1], {"tile": up}),
            remote(window, xw.at[pl.ds(0, ROWS), pl.ds(lane0, 512)], hsend.at[1], hrecv.at[0], {"tile": down}),
        )
    )
    fb[0] = zs[:, pl.ds(pl.multiple_of(LOW * c, LOW), LOW)]
    hp[0] = zp[c]

    high_cols = CHUNK * FRAMES
    load_x.wait()
    halo.wait_recv()
    row = ROWS * t - ROWS + iota((3 * ROWS, 512), 0)
    col = CHUNK * c - 128 + iota((3 * ROWS, 512), 1)
    inside = (row >= 0) & (row < ROWS * tiles) & (col >= 0) & (col < high_cols)
    raw = jnp.where(inside, xw[:, 128:640], 0.0)
    lane_in = iota((512, 256), 0)
    lane_out = iota((512, 256), 1)
    for phase in range(2):
        table = jnp.where(lane_in == 96 + phase + 2 * lane_out, 1.0, 0.0).astype(BF16)
        xs[phase] = pick(raw, table)

    row = ROWS * t - ROWS + iota((3 * ROWS, 256), 0)
    col = CHUNK * c - 32 + 2 * iota((3 * ROWS, 256), 1)
    inside = (row >= 0) & (row < ROWS * tiles) & (col >= 0) & (col < high_cols)
    gain = jnp.where(inside, 2.0, 1.0)
    pg[0] = left(gain, -1)
    pg[1] = gain
    pg[2] = left(gain, 1)

    def split(value):
        high = value.astype(BF16)
        return high, (value - high.astype(F32)).astype(BF16)

    def stage_model(lo):
        for off in range(OFFS):
            rows = slice(BAND * off, BAND * off + BAND)
            xh[rows], xl[rows] = split(left(xs[off % 2, lo : lo + BAND], off // 2))

    def stage_prior(lo, count):
        for phase in range(2):
            double = 2.0 * xs[phase, lo : lo + count]
            px[3 * phase, lo : lo + count] = left(double, -1)
            px[3 * phase + 1, lo : lo + count] = double
            px[3 * phase + 2, lo : lo + count] = left(double, 1)

    def prior(phase, lo, count):
        centre = px[3 * phase + 1, lo : lo + count]
        total = jnp.zeros((count, 256), F32)
        for side in range(-WINDOW, WINDOW + 1):
            other = (phase + side) % 2
            lanes = (phase + side - other) // 2 + 1
            for down_off in range(-WINDOW, WINDOW + 1):
                if down_off == 0 and side == 0:
                    continue
                rows = slice(lo + down_off, lo + down_off + count)
                weight = 0.7 ** (abs(down_off) + abs(side))
                slope = jnp.tanh(centre - px[3 * other + lanes, rows])
                total = total + (weight * slope) * pg[lanes, rows]
        return total

    xh[OFFS * BAND : KDIM] = jnp.zeros((KDIM - OFFS * BAND, 256), BF16)
    xl[OFFS * BAND : KDIM] = jnp.zeros((KDIM - OFFS * BAND, 256), BF16)
    aa[OFFS * BAND : KDIM] = jnp.zeros((KDIM - OFFS * BAND, 128), F32)
    stage_model(REACH)

    for copy in scopies.values():
        copy.wait_recv()
    frame = iota((1, 128), 1) // 8
    down_shift = jnp.zeros((1, 128), F32)
    side_shift = jnp.zeros((1, 128), F32)
    for slot in range(FRAMES):
        down_shift = jnp.where(frame == slot, hp[slot, 0:1, 2 * EDGE : 2 * EDGE + 1], down_shift)
        side_shift = jnp.where(frame == slot, hp[slot, 0:1, 2 * EDGE + 1 : 2 * EDGE + 2], side_shift)
        rows = jnp.where(
            sub < 4, jnp.broadcast_to(hp[slot, 0:1], (8, 128)), jnp.broadcast_to(hp[slot, 1:2], (8, 128))
        )
        for _ in range(2):
            rows = pltpu.roll(rows, 0, 1, stride=SLOT // 2, stride_axis=0)
        fh[8 * slot : 8 * slot + 8] = rows
    load_b.wait()
    blur_sum = taps_in[0]
    for tap in range(1, TAPS):
        blur_sum = blur_sum + taps_in[tap]
    scale = jnp.full((1, 128), blur_sum)
    taps = [jnp.full((1, 128), taps_in[tap]) / scale for tap in range(TAPS)]

    def tap_at(distance):
        total = jnp.zeros(distance.shape, F32)
        for tap in range(TAPS):
            total = jnp.where(distance == float(tap - RADIUS), jnp.broadcast_to(taps[tap], distance.shape), total)
        return total

    place = (iota((BAND, 128), 0) - REACH - 2 * (iota((BAND, 128), 1) % 8)).astype(F32)
    by_row = tap_at(place - down_shift)
    by_col = tap_at((iota((24, 128), 0) - REACH).astype(F32) - side_shift)
    for off in range(OFFS):
        rows = slice(BAND * off, BAND * off + BAND)
        entry = by_row * by_col[off : off + 1]
        aa[rows] = entry
        high, rest = split(entry)
        for place_at, group in enumerate(GROUPS):
            into = slice(GROUP * place_at + 8 * off, GROUP * place_at + 8 * off + 8)
            of = slice(8 * group, 8 * group + 8)
            a3[into, 0:128] = high[of]
            a3[into, 128:256] = rest[of]
            a3[into, 256:384] = high[of]
    for place_at in range(4):
        a3[GROUP * place_at + 8 * OFFS : GROUP * place_at + GROUP] = jnp.zeros((8, 384), BF16)
    for block in range(KDIM // 128):
        columns = slice(128 * block, 128 * block + 128)
        af[:128, columns], af[128:, columns] = split(aa[128 * block : 128 * block + 128].T)

    low = LOW * c - EDGE + iota((128, 256), 1)
    live = (low >= 0) & (low < LOW * FRAMES)

    def misfits():
        both = jnp.dot(af[...], xh[...], preferred_element_type=F32)
        return both[:128] + both[128:] + jnp.dot(af[:128], xl[...], preferred_element_type=F32)

    def adjoint(pred):
        seen = jnp.concatenate([fb[...].reshape(128, LOW), fh[...]], axis=1)
        high, rest = split(jnp.where(live, jnp.tanh(pred - seen), 0.0))
        return jnp.concatenate([high, high, rest], axis=0)

    def spread(first_at, count, gap, move, width):
        rows = slice(GROUP * first_at, GROUP * (first_at + count))
        hh[rows] = jnp.dot(a3[rows], gap, preferred_element_type=F32)
        sums = {}
        for place_at in range(first_at, first_at + count):
            for phase in range(2):
                total = jnp.zeros((8, width), F32)
                for off in range(phase, OFFS, 2):
                    at = GROUP * place_at + 8 * off
                    total = total + left(hh[at : at + 8], move - off // 2)[:, :width]
                sums[GROUPS[place_at], phase] = total
        return sums

    pred = misfits()
    for copy in fcopies.values():
        copy.wait_recv()
    gap = adjoint(pred)
    first = across_tiles(
        remote(d1.at[:, pl.ds(0, ROWS)], r1.at[:, pl.ds(ROWS, ROWS)], e1send.at[0], e1recv.at[1], {"tile": up}),
        remote(d1.at[:, pl.ds(ROWS, ROWS)], r1.at[:, pl.ds(0, ROWS)], e1send.at[1], e1recv.at[0], {"tile": down}),
    )
    for (group, phase), total in spread(0, 2, gap, 0, 256).items():
        d1[phase, 8 * group : 8 * group + 8] = total
    pl.when(t > 0)(first.above.start)
    for (group, phase), total in spread(2, 2, gap, 0, 256).items():
        d1[phase, 8 * group : 8 * group + 8] = total
    pl.when(t < tiles - 1)(first.below.start)
    started.append(first)
    reach_row = ROWS * t - REACH + iota((BAND, 256), 0)
    edge_row = (reach_row < REACH) | (reach_row >= ROWS * tiles - REACH)
    within = pg[1, REACH : REACH + BAND] > 1.5
    stage_prior(0, 3 * ROWS)
    for phase in range(2):
        pr[phase] = xs[phase, REACH : REACH + BAND] - 0.005 * prior(phase, REACH, BAND)
    first.wait_recv()
    for phase in range(2):
        theirs = jnp.where(edge_row, 0.0, r1[phase])
        xs[phase, REACH : REACH + BAND] = jnp.where(within, pr[phase] - 0.1 * (d1[phase] + theirs), 0.0)

    stage_model(REACH)
    gap = adjoint(misfits())
    for (group, phase), total in spread(1, 2, gap, ROWS, LOW).items():
        d2[group // 3, phase] = total
    second = go(
        across_tiles(
            remote(d2.at[0], r2.at[1], e2send.at[0], e2recv.at[1], {"tile": up}),
            remote(d2.at[1], r2.at[0], e2send.at[1], e2recv.at[0], {"tile": down}),
        )
    )

    inner = spread(0, 1, gap, ROWS, LOW) | spread(3, 1, gap, ROWS, LOW)
    both = [jnp.concatenate([inner[1, phase], inner[2, phase]], axis=0) for phase in range(2)]
    stage_prior(REACH, BAND)
    for phase in range(2):
        kept = xs[phase, ROWS : 2 * ROWS] - 0.005 * prior(phase, ROWS, ROWS)
        both[phase] = left(kept, ROWS)[:, :128] - 0.1 * both[phase]
    lane_in = iota((CHUNK, CHUNK), 0)
    lane_out = iota((CHUNK, CHUNK), 1)
    table = jnp.where(lane_out == jnp.where(lane_in < LOW, 2 * lane_in, 2 * lane_in - CHUNK + 1), 1.0, 0.0).astype(BF16)
    own_row = ROWS * t + iota((ROWS, LOW), 0)
    edge_row = (own_row < REACH) | (own_row >= ROWS * tiles - REACH)
    second.wait_recv()
    halves = []
    for phase in range(2):
        theirs = jnp.concatenate([r2[0, phase], r2[1, phase]], axis=0)
        halves.append(both[phase] - 0.1 * jnp.where(edge_row, 0.0, theirs))
    result = pick(jnp.concatenate(halves, axis=1), table)

    mine[...] = result
    own = out.at[:, pl.ds(pl.multiple_of(CHUNK * c, CHUNK), CHUNK)]
    keep = pltpu.make_async_copy(mine, own, load_sem.at[4])
    def gather(slot, source, target, device):
        return remote(source, target, gsend.at[slot], grecv.at[slot], device)

    direct = [gather(slot, mine, own, peer(slot)[0]) for slot in order]

    relays = (t % 2 == 1) & (t != tiles // 2 - 1)
    @pl.when(jnp.logical_not(relays))
    def _():
        for copy in direct:
            copy.start()
        keep.start()
        for copy in direct:
            copy.wait_recv()
        for copy in direct:
            copy.wait_send()

    @pl.when(relays)
    def _():
        copies = {slot: copy for slot, copy in zip(order, direct) if slot < SIDE or slot % SIDE == 0}
        for slot in (2, 1, 3, 8, 4, 12):
            copies[slot].start()
        keep.start()
        for ey in (1, 3, 2):
            copies[ey].wait_recv()
            source = SIDE * lax.rem(y + SIDE - ey, SIDE) + x
            passing = out.at[:, pl.ds(pl.multiple_of(CHUNK * source, CHUNK), CHUNK)]
            for ex in (2, 1, 3):
                slot = SIDE * ex + ey
                copies[slot] = gather(slot, passing, passing, peer(SIDE * ex)[0])
                copies[slot].start()
        for slot, copy in copies.items():
            if slot >= SIDE:
                copy.wait_recv()
        for copy in copies.values():
            copy.wait_send()

    keep.wait()
    for copy in started:
        copy.wait_send()


def local(tiles, estimate, frames, shifts, blur):
    vmem = lambda *shape: pltpu.VMEM(shape, F32)
    dma = lambda n: pltpu.SemaphoreType.DMA((n,))
    return pl.pallas_call(
        functools.partial(kernel, tiles),
        out_shape=jax.ShapeDtypeStruct(estimate.shape, F32),
        in_specs=[pl.BlockSpec(memory_space=pltpu.HBM)] * 4,
        out_specs=pl.BlockSpec(memory_space=pl.ANY),
        scratch_shapes=[
            pltpu.SMEM((TAPS,), F32),
            pltpu.SMEM((1, 2), jnp.int32),
            vmem(3 * ROWS, 768),
            vmem(8, FRAMES * LOW),
            vmem(8, FRAMES * LOW + 128),
            vmem(FRAMES, 2, 128),
            vmem(FRAMES, 8, LOW),
            vmem(FRAMES, 2, 128),
            vmem(128, 128),
            vmem(2, 3 * ROWS, 256),
            vmem(6, 3 * ROWS, 256),
            vmem(3, 3 * ROWS, 256),
            pltpu.VMEM((KDIM, 256), BF16),
            pltpu.VMEM((KDIM, 256), BF16),
            vmem(KDIM, 128),
            pltpu.VMEM((4 * GROUP, 384), BF16),
            pltpu.VMEM((256, KDIM), BF16),
            vmem(4 * GROUP, 256),
            vmem(2, BAND, 256),
            vmem(2, BAND, 256),
            vmem(2, 2, REACH, 128),
            vmem(2, 2, REACH, 128),
            vmem(2, BAND, 256),
            vmem(ROWS, CHUNK),
            dma(5), dma(2), dma(2), dma(FRAMES), dma(FRAMES), dma(FRAMES), dma(FRAMES),
            dma(2), dma(2), dma(2), dma(2), dma(FRAMES), dma(FRAMES),
        ],
        compiler_params=pltpu.CompilerParams(collective_id=0, has_side_effects=True, vmem_limit_bytes=16 * 1024 * 1024),
    )(*(pltpu.with_memory_space_constraint(value, pltpu.HBM) for value in (estimate, frames, shifts, blur)))


def solution(mesh):
    placed = (P("tile", None), P("frame", "tile", None), P("frame", None), P())
    return jax.shard_map(
        functools.partial(local, mesh.shape["tile"]),
        mesh=mesh, in_specs=placed, out_specs=P("tile", None), check_vma=False,
    )
```
